32 devices in a mesh: tm: 4 (over y, core), head: 2 (over x), branch: 4 (over z).
Axes of the slice: x: 2, y: 2, z: 4, core: 2. Of those that a mesh axis runs over, the one named last changes fastest.
Arguments:
- queries: bfloat16 [4, 4, 512, 20, 128], P('branch', 'tm', 'head'), may hold values from -8 to 8
- keys: bfloat16 [4, 4, 512, 20, 128], P('branch', 'tm', 'head'), may hold values from -5 to 5
- values: bfloat16 [4, 4, 512, 20, 128], P('branch', 'tm', 'head'), may hold values from -6 to 6
- ctx_keys: bfloat16 [4, 512, 20, 128], P('tm', ('head', 'branch')), may hold values from -5 to 5
- ctx_values: bfloat16 [4, 512, 20, 128], P('tm', ('head', 'branch')), may hold values from -6 to 6
- hidden: bfloat16 [4, 4, 512, 5120], P('branch', 'tm', 'head'), may hold values from -6 to 6
- out_weight: bfloat16 [2560, 5120], P('head'), may hold values from -0.5 to 0.5
- gates: float32 [16, 5120], replicated, may hold values from 0.5 to 2
- levels: int32 [4], replicated, may hold values from 0 to 15
- span_mask: int32 [4, 4], replicated, may hold values from 0 to 1, as said below
- prefix: int32 [1], replicated, may hold values from 1 to 3
Outputs:
- updated: bfloat16 [4, 4, 512, 5120], P('branch', 'tm', 'head')
The draws below stay inside these ranges and needn't reach their ends.
Inputs may be any that keep to these rules, and one draw needn't show every extreme that they name: `span_mask`: 1 on the diagonal and in the first column, 0 above the diagonal.
All inputs are finite; a program needn't handle non-finite values.
Results may differ from the reference program's by a relative error of at most 0.01.
Values may be sent and summed in bfloat16 or wider, within the bound.
No kernel may reach another device: no remote copies, remote signals or barrier semaphores. Data moves between devices by JAX's collectives and lax.ppermute only.
A program may use at most 256 MiB of HBM per device.

```python
import math
import jax
import jax.numpy as jnp
from jax import lax

D = 5120
H = 20
HD = 128
TOK = 512
LEVELS = 16
SPANS = 4
BRANCHES = 4
HEAD_GROUP = 10


def draw_keys(key, part):
    base_draw = jax.random.normal(jax.random.fold_in(key, 21), (BRANCHES, SPANS, TOK, H, HD), jnp.float32)
    return jnp.clip(base_draw, -5.0, 5.0).astype(jnp.bfloat16)


def draw_queries(key, part):
    base_draw = jax.random.normal(jax.random.fold_in(key, 31), (BRANCHES, SPANS, TOK, H, HD), jnp.float32)
    base_draw = 2.0 * base_draw
    return jnp.clip(base_draw, -8.0, 8.0).astype(jnp.bfloat16)


def draw_span_mask(key, part):
    coins = jax.random.randint(jax.random.fold_in(key, 41), (SPANS, SPANS), 0, 4)
    row_ids = jnp.arange(SPANS, dtype=jnp.int32)[:, None]
    col_ids = jnp.arange(SPANS, dtype=jnp.int32)[None, :]
    keep_cell = (col_ids < row_ids) & (coins > 0) | (col_ids == row_ids) | (col_ids == 0)
    return keep_cell.astype(jnp.int32)


def set_ends(result, rng, low, high):
    place = [jax.random.randint(jax.random.fold_in(rng, axis), (), 0, length) for axis, length in enumerate(result.shape)]
    widest = result.shape.index(max(result.shape))
    beside = place[:widest] + [(place[widest] + 1) % result.shape[widest]] + place[widest + 1:]
    return result.at[tuple(place)].set(low).at[tuple(beside)].set(high)


def steps_of(key, extent, shards, least, high):
    loudness, own = 1.0, jax.random.fold_in(key, 6)
    for axis_at, blocks in shards:
        heights = jnp.exp(jax.random.uniform(jax.random.fold_in(own, axis_at), (blocks,), jnp.float32, least / len(shards), high / len(shards)))
        loudness = loudness * jnp.repeat(heights, extent[axis_at] // blocks).reshape([-1 if axis == axis_at else 1 for axis in range(len(extent))])
    return loudness


def scatter_about(rng, dims, spread, reach, pieces=(), held_as=jnp.bfloat16):
    entries = jax.random.normal(rng, dims, jnp.float32) * spread
    if len(pieces) > 0:
        entries = steps_of(rng, dims, pieces, -0.22, 0.18) * entries
    return jnp.clip(entries, min=-reach, max=reach).astype(held_as)


def setup_inputs(seed: int = 0) -> dict:
    splits = jax.random.split(jax.random.key(seed), 12)
    return {
        "queries": draw_queries(jax.random.fold_in(splits[11], 71), 0),
        "keys": draw_keys(jax.random.fold_in(splits[11], 71), 0),
        "values": scatter_about(splits[2], (BRANCHES, SPANS, TOK, H, HD), 1.0, 6.0, ((0, 4), (1, 4), (2, 2))),
        "ctx_keys": scatter_about(splits[3], (SPANS, TOK, H, HD), 1.0, 5.0, ((0, 4), (1, 8))),
        "ctx_values": scatter_about(splits[4], (SPANS, TOK, H, HD), 1.0, 6.0, ((0, 4), (1, 8))),
        "hidden": scatter_about(splits[5], (BRANCHES, SPANS, TOK, D), 1.0, 6.0, ((0, 4), (1, 4), (2, 2))),
        "out_weight": scatter_about(splits[6], (H * HD, D), HD ** -0.5, 0.5, ((0, 2),)),
        "gates": jnp.clip(jax.random.uniform(splits[7], (LEVELS, D), jnp.float32, 0.5, 2.0), 0.5, 2.0),
        "levels": set_ends(jax.random.randint(splits[8], (SPANS,), 0, LEVELS), jax.random.fold_in(splits[8], 1), 0, LEVELS - 1).astype(jnp.int32),
        "span_mask": draw_span_mask(jax.random.fold_in(splits[11], 71), 0),
        "prefix": jax.random.randint(splits[10], (1,), 1, SPANS).astype(jnp.int32),
    }


NEG_BIG = -1e+30

def reference(queries, keys, values, ctx_keys, ctx_values, hidden, out_weight, gates, levels, span_mask, prefix):
    score_scale = 1.0 / math.sqrt(HD)
    use_context = jnp.arange(SPANS, dtype=jnp.int32) < prefix[0]
    weight_groups = out_weight.reshape(H // HEAD_GROUP, HEAD_GROUP, HD, D).astype(jnp.float32)

    def one_slot(slot_index):
        branch_index = slot_index // SPANS
        span_index = slot_index % SPANS
        branch_keys = lax.dynamic_index_in_dim(keys, branch_index, 0, keepdims=False)
        branch_values = lax.dynamic_index_in_dim(values, branch_index, 0, keepdims=False)
        slot_keys = jnp.where(use_context[:, None, None, None], ctx_keys, branch_keys).reshape(SPANS * TOK, H, HD)
        slot_values = jnp.where(use_context[:, None, None, None], ctx_values, branch_values).reshape(SPANS * TOK, H, HD)
        mask_row = lax.dynamic_index_in_dim(span_mask, span_index, 0, keepdims=False)
        visible = jnp.repeat(mask_row > 0, TOK)
        branch_queries = lax.dynamic_index_in_dim(queries, branch_index, 0, keepdims=False)
        span_queries = lax.dynamic_index_in_dim(branch_queries, span_index, 0, keepdims=False)

        def one_head(head_index):
            head_q = lax.dynamic_index_in_dim(span_queries, head_index, 1, keepdims=False)
            head_k = lax.dynamic_index_in_dim(slot_keys, head_index, 1, keepdims=False)
            head_v = lax.dynamic_index_in_dim(slot_values, head_index, 1, keepdims=False)
            scores = jnp.dot(head_q, head_k.T, preferred_element_type=jnp.float32) * score_scale
            row_max = lax.optimization_barrier(jnp.max(jnp.where(visible[None, :], scores, NEG_BIG), axis=1))
            exp_terms = jnp.where(visible[None, :], jnp.exp(scores - row_max[:, None]), 0.0)
            denominator = lax.optimization_barrier(jnp.sum(exp_terms, axis=1))
            summed = jnp.dot(exp_terms.astype(jnp.bfloat16), head_v, preferred_element_type=jnp.float32)
            return (summed / denominator[:, None]).astype(jnp.bfloat16)
        attended = lax.map(one_head, jnp.arange(H, dtype=jnp.int32))
        grouped = attended.reshape(H // HEAD_GROUP, HEAD_GROUP, TOK, HD).astype(jnp.float32)
        partial_value = jnp.einsum('gaqd,gadn->gqn', grouped, weight_groups).astype(jnp.bfloat16)
        partial_value = lax.optimization_barrier(partial_value)
        projected = lax.optimization_barrier(jnp.sum(partial_value.astype(jnp.float32), axis=0))
        level_now = lax.dynamic_index_in_dim(levels, span_index, 0, keepdims=False)
        gate_row = lax.dynamic_index_in_dim(gates, level_now, 0, keepdims=False)
        branch_hidden = lax.dynamic_index_in_dim(hidden, branch_index, 0, keepdims=False)
        span_hidden = lax.dynamic_index_in_dim(branch_hidden, span_index, 0, keepdims=False)
        return (span_hidden.astype(jnp.float32) + gate_row[None, :] * projected).astype(jnp.bfloat16)
    updated = lax.map(one_slot, jnp.arange(BRANCHES * SPANS, dtype=jnp.int32))
    return updated.reshape(BRANCHES, SPANS, TOK, D)
```

```python
import functools
import math

import jax
import jax.numpy as jnp
from jax import lax
from jax.experimental import pallas as pl
from jax.experimental.pallas import tpu as pltpu
from jax.sharding import PartitionSpec as P

NEG_BIG = -1e30
LOG2E = 1.4426950408889634
COL_BLOCKS = 4


def flash_kernel(flags, *refs, chunks, scale):
    q_ref = refs[0]
    kv_refs = refs[1 : 1 + len(chunks)]
    out_ref, max_ref, sum_ref, acc_ref = refs[1 + len(chunks) :]
    max_ref[...] = jnp.full_like(max_ref, NEG_BIG)
    sum_ref[...] = jnp.zeros_like(sum_ref)
    acc_ref[...] = jnp.zeros_like(acc_ref)
    for kv_ref, flag in zip(kv_refs, chunks):

        @pl.when(flags[flag] > 0)
        def _(kv_ref=kv_ref):
            q = q_ref[0]
            raw = lax.dot_general(
                q, kv_ref[0, 0], (((1,), (1,)), ((), ())), preferred_element_type=jnp.float32
            )
            old_max = max_ref[...]
            new_max = jnp.maximum(old_max, jnp.max(raw, axis=1, keepdims=True))
            weights = jnp.exp2((raw - new_max) * scale)
            shrink = jnp.exp2((old_max - new_max) * scale)
            max_ref[...] = new_max
            sum_ref[...] = sum_ref[...] * shrink + jnp.sum(weights, axis=1, keepdims=True)
            acc_ref[...] = acc_ref[...] * shrink + jnp.dot(
                weights.astype(jnp.bfloat16), kv_ref[1, 0], preferred_element_type=jnp.float32
            )

    out_ref[...] = (acc_ref[...] / sum_ref[...]).astype(out_ref.dtype)


def attend(queries, chunks, flags):
    heads, rows, dim = queries.shape
    arrays = [array for array, _ in chunks]
    keys = sum(array.shape[2] for array in arrays)
    return pl.pallas_call(
        functools.partial(
            flash_kernel,
            chunks=tuple(flag for _, flag in chunks),
            scale=LOG2E / math.sqrt(dim),
        ),
        out_shape=jax.ShapeDtypeStruct((rows, heads * dim), jnp.bfloat16),
        grid_spec=pltpu.PrefetchScalarGridSpec(
            num_scalar_prefetch=1,
            grid=(heads,),
            in_specs=[pl.BlockSpec((1, rows, dim), lambda h, f: (h, 0, 0))]
            + [
                pl.BlockSpec((2, 1, array.shape[2], dim), lambda h, f: (0, h, 0, 0))
                for array in arrays
            ],
            out_specs=pl.BlockSpec((rows, dim), lambda h, f: (0, h)),
            scratch_shapes=[
                pltpu.VMEM((rows, 1), jnp.float32),
                pltpu.VMEM((rows, 1), jnp.float32),
                pltpu.VMEM((rows, dim), jnp.float32),
            ],
        ),
        cost_estimate=pl.CostEstimate(
            flops=4 * heads * rows * keys * dim,
            bytes_accessed=2 * heads * dim * (2 * rows + 2 * keys),
            transcendentals=heads * rows * keys,
        ),
    )(flags, queries, *arrays)


def body(sizes, queries, keys, values, ctx_keys, ctx_values, hidden, out_weight, gates, levels, span_mask, prefix):
    spans, splits, branches = sizes
    span = lax.axis_index("tm")
    part = lax.axis_index("head")
    to_heads = lambda a: jnp.transpose(a, (1, 0, 2))
    q = to_heads(queries[0, 0])
    k, v = to_heads(keys[0, 0]), to_heads(values[0, 0])
    ck, cv = to_heads(ctx_keys[0]), to_heads(ctx_values[0])
    group = q.shape[0] // splits
    take = lambda a, d: lax.dynamic_slice_in_dim(a, lax.rem(part + d, splits) * group, group, 0)
    send = lambda a, d: lax.ppermute(a, "head", [(i, (i + d) % splits) for i in range(splits)])

    ctx_parts = [jnp.stack([take(ck, 0), take(cv, 0)])]
    kv_parts = [jnp.stack([take(k, 0), take(v, 0)])]
    q_parts = [take(q, 0)]
    for d in range(1, splits):
        ctx_parts.append(send(jnp.stack([take(ck, d), take(cv, d)]), d))
    for d in range(1, splits):
        kv_parts.append(send(jnp.stack([take(k, d), take(v, d)]), d))
    for d in range(1, splits):
        q_parts.append(send(take(q, d), d))

    ctx_own = jnp.concatenate(ctx_parts, axis=2)
    ctx_pieces = [ctx_own]
    for d in range(1, branches):
        ctx_pieces.append(
            lax.ppermute(ctx_own, "branch", [(i, (i + d) % branches) for i in range(branches)])
        )
    piece = ctx_own.shape[2]
    rows = k.shape[1]
    per_part = rows // piece
    use_context = span < prefix[0]
    own = []
    for d in range(splits):
        ctx_chunk = jnp.concatenate(ctx_pieces[d * per_part : (d + 1) * per_part], axis=2)
        own.append(jnp.where(use_context, ctx_chunk, kv_parts[d]))

    swap_up = [(i, i + 1) for i in range(0, spans, 2)]
    swap = swap_up + [(i + 1, i) for i in range(0, spans, 2)]
    mask_row = lax.dynamic_index_in_dim(span_mask, span, 0, keepdims=False)
    seen = lambda s: jnp.where(
        (s >= 0) & (s < spans), mask_row[jnp.clip(s, 0, spans - 1)], 0
    ).astype(jnp.int32)
    partner = span + 1 - 2 * lax.rem(span, 2)
    flags = [jnp.int32(1), jnp.where(partner < span, seen(partner), 0)]
    chunks = [(a, 0) for a in own]
    chunks += [(lax.ppermute(a, "tm", swap_up), 1) for a in own]
    for s in range(2, spans, 2):
        far = [lax.ppermute(a, "tm", [(i, i + s) for i in range(spans - s)]) for a in own]
        chunks += [(a, len(flags)) for a in far]
        flags.append(seen(span - s))
        chunks += [(lax.ppermute(a, "tm", swap), len(flags)) for a in far]
        flags.append(seen(partner - s))
    flags = jnp.stack(flags)

    columns = out_weight.shape[1]
    width = columns // COL_BLOCKS
    project = lambda a, j: jnp.dot(
        a, out_weight[:, j * width : (j + 1) * width], preferred_element_type=jnp.float32
    ).astype(jnp.bfloat16)
    returned = [[] for _ in range(COL_BLOCKS)]
    q_own = q_parts[0]
    for d in range(1, splits):
        attended = attend(q_parts[d], chunks, flags)
        for j in range(COL_BLOCKS):
            returned[j].append(
                lax.ppermute(project(attended, j), "head", [((i + d) % splits, i) for i in range(splits)])
            )
        q_own, attended = lax.optimization_barrier((q_own, attended))
    attended = attend(q_own, chunks, flags)
    level_now = lax.dynamic_index_in_dim(levels, span, 0, keepdims=False)
    gate_row = lax.dynamic_index_in_dim(gates, level_now, 0, keepdims=False)
    outs = []
    for j in range(COL_BLOCKS):
        cols = slice(j * width, (j + 1) * width)
        total = project(attended, j).astype(jnp.float32)
        for a in returned[j]:
            total = total + a.astype(jnp.float32)
        outs.append(
            (hidden[0, 0][:, cols].astype(jnp.float32) + gate_row[None, cols] * total).astype(jnp.bfloat16)
        )
    return jnp.concatenate(outs, axis=1)[None, None]


def solution(mesh):
    sizes = (mesh.shape["tm"], mesh.shape["head"], mesh.shape["branch"])
    return jax.shard_map(
        functools.partial(body, sizes),
        mesh=mesh,
        in_specs=(
            P("branch", "tm", "head", None, None),
            P("branch", "tm", "head", None, None),
            P("branch", "tm", "head", None, None),
            P("tm", ("head", "branch"), None, None),
            P("tm", ("head", "branch"), None, None),
            P("branch", "tm", "head", None),
            P("head", None),
            P(),
            P(),
            P(),
            P(),
        ),
        out_specs=P("branch", "tm", "head", None),
        check_vma=False,
    )
```

```python
import functools
import math

import jax
import jax.numpy as jnp
from jax import lax
from jax.experimental import pallas as pl
from jax.experimental.pallas import tpu as pltpu
from jax.sharding import PartitionSpec as P

NEG_BIG = -1e30
LOG2E = 1.4426950408889634
COL_BLOCKS = 4
HEAD_STEP_SCORES = 3 << 20
VMEM_LIMIT = 60 << 20


def flash_kernel(flags, *refs, spans, scale, step):
    count = sum(len(members) for _, members in spans)
    q_ref, kv_refs = refs[0], refs[1 : 1 + count]
    out_ref, score_ref, max_ref, sum_ref, acc_ref = refs[1 + count :]
    dim = q_ref.shape[2]
    max_ref[...] = jnp.full_like(max_ref, NEG_BIG)
    sum_ref[...] = jnp.zeros_like(sum_ref)
    acc_ref[...] = jnp.zeros_like(acc_ref)
    start = 0
    offsets = []
    for _, members in spans:
        offsets.append(start)
        start += sum(kv_refs[i].shape[2] for i in members)
    for (flag, members), base in zip(spans, offsets):

        @pl.when(flags[flag] > 0)
        def _(members=members, base=base):
            for h in range(step):
                block = jnp.concatenate([kv_refs[i][0, h] for i in members], axis=0)
                raw = lax.dot_general(
                    q_ref[h], block, (((1,), (1,)), ((), ())), preferred_element_type=jnp.float32
                )
                score_ref[h, :, base : base + block.shape[0]] = raw
                top = max_ref[h]
                for j in range(0, block.shape[0], dim):
                    top = jnp.maximum(top, raw[:, j : j + dim])
                max_ref[h] = top

    for h in range(step):
        row_max = jnp.max(max_ref[h], axis=1, keepdims=True)
        max_ref[h] = jnp.broadcast_to(row_max * scale, max_ref.shape[1:])
    for (flag, members), base in zip(spans, offsets):

        @pl.when(flags[flag] > 0)
        def _(members=members, base=base):
            for h in range(step):
                block = jnp.concatenate([kv_refs[i][1, h] for i in members], axis=0)
                top, total = max_ref[h], sum_ref[h]
                weights = []
                for j in range(0, block.shape[0], dim):
                    part = jnp.exp2(score_ref[h, :, base + j : base + j + dim] * scale - top)
                    total = total + part
                    weights.append(part.astype(jnp.bfloat16))
                sum_ref[h] = total
                acc_ref[h] = acc_ref[h] + jnp.dot(
                    jnp.concatenate(weights, axis=1), block, preferred_element_type=jnp.float32
                )

    for h in range(step):
        total = jnp.sum(sum_ref[h], axis=1, keepdims=True)
        out_ref[:, h * dim : (h + 1) * dim] = (acc_ref[h] / total).astype(out_ref.dtype)


def attend(queries, spans, flags):
    heads, rows, dim = queries.shape
    arrays, layout = [], []
    for flag, members in spans:
        layout.append((flag, tuple(range(len(arrays), len(arrays) + len(members)))))
        arrays += members
    keys = sum(array.shape[2] for array in arrays)
    step = max(s for s in range(1, heads + 1) if heads % s == 0 and s * rows * keys <= HEAD_STEP_SCORES)
    wide = pltpu.VMEM((step, rows, dim), jnp.float32)
    return pl.pallas_call(
        functools.partial(
            flash_kernel, spans=tuple(layout), scale=LOG2E / math.sqrt(dim), step=step
        ),
        out_shape=jax.ShapeDtypeStruct((rows, heads * dim), jnp.bfloat16),
        grid_spec=pltpu.PrefetchScalarGridSpec(
            num_scalar_prefetch=1,
            grid=(heads // step,),
            in_specs=[pl.BlockSpec((step, rows, dim), lambda h, f: (h, 0, 0))]
            + [
                pl.BlockSpec((2, step, array.shape[2], dim), lambda h, f: (0, h, 0, 0))
                for array in arrays
            ],
            out_specs=pl.BlockSpec((rows, step * dim), lambda h, f: (0, h)),
            scratch_shapes=[pltpu.VMEM((step, rows, keys), jnp.float32), wide, wide, wide],
        ),
        cost_estimate=pl.CostEstimate(
            flops=4 * heads * rows * keys * dim,
            bytes_accessed=2 * heads * dim * (2 * rows + 2 * keys),
            transcendentals=heads * rows * keys,
        ),
        compiler_params=pltpu.CompilerParams(vmem_limit_bytes=VMEM_LIMIT),
    )(flags, queries, *arrays)


def body(sizes, queries, keys, values, ctx_keys, ctx_values, hidden, out_weight, gates, levels, span_mask, prefix):
    return sublayer(
        sizes, queries[0, 0], keys[0, 0], values[0, 0], ctx_keys[0], ctx_values[0], hidden[0, 0],
        out_weight, gates, levels, span_mask, prefix,
    )[None, None]


def permute(array, axis, pairs):
    return lax.ppermute(array, axis, pairs)


def sublayer(sizes, queries, keys, values, ctx_keys, ctx_values, hidden, out_weight, gates, levels, span_mask, prefix):
    spans, splits, branches = sizes
    span = lax.axis_index("tm")
    part = lax.axis_index("head")
    branch = lax.axis_index("branch")
    to_heads = lambda a: jnp.transpose(a, (1, 0, 2))
    q, k, v = to_heads(queries), to_heads(keys), to_heads(values)
    ck, cv = to_heads(ctx_keys), to_heads(ctx_values)
    group = q.shape[0] // splits
    take = lambda a, d: lax.dynamic_slice_in_dim(a, lax.rem(part + d, splits) * group, group, 0)
    pair = lambda a, b, d: jnp.stack([take(a, d), take(b, d)])
    cycle = lambda d: [(i, (i + d) % splits) for i in range(splits)]

    ctx_parts, kv_parts, q_parts = [pair(ck, cv, 0)], [pair(k, v, 0)], [take(q, 0)]
    for d in range(1, splits):
        ctx_parts.append(permute(pair(ck, cv, d), "head", cycle(d)))
    for d in range(1, splits):
        kv_parts.append(permute(pair(k, v, d), "head", cycle(d)))
    for d in range(1, splits):
        q_parts.append(permute(take(q, d), "head", cycle(d)))

    ctx_pieces = [jnp.concatenate(ctx_parts, axis=2)]
    up, down = [ctx_pieces[0]], [ctx_pieces[0]]
    for s in range(1, branches):
        up.append(permute(up[-1], "branch", [(i, i + 1) for i in range(s - 1, branches - 1)]))
        down.append(permute(down[-1], "branch", [(i, i - 1) for i in range(1, branches - s + 1)]))
        piece = up[s]
        for t in range(1, s + 1):
            piece = jnp.where(branch == s - t, down[t], piece)
        ctx_pieces.append(piece)

    use_context = span < prefix[0]
    piece_rows, rows = ctx_pieces[0].shape[2], k.shape[1]
    own = []
    for j, ctx_piece in enumerate(ctx_pieces):
        d, at = divmod(j * piece_rows, rows)
        if own:
            _, ctx_piece = lax.optimization_barrier((own[-1], ctx_piece))
        own.append(jnp.where(use_context, ctx_piece, kv_parts[d][:, :, at : at + piece_rows]))

    swap_up = [(i, i + 1) for i in range(0, spans, 2)]
    swap = swap_up + [(i + 1, i) for i in range(0, spans, 2)]
    mask_row = lax.dynamic_index_in_dim(span_mask, span, 0, keepdims=False)
    ids = jnp.arange(spans, dtype=jnp.int32)
    seen = lambda s: jnp.sum(jnp.where((ids == s) & (ids <= span), mask_row, 0))
    partner = span + 1 - 2 * lax.rem(span, 2)
    flags = [jnp.int32(1), seen(partner)]
    groups = [own, []]
    for s in range(2, spans, 2):
        groups += [[], []]
        flags += [seen(span - s), seen(partner - s)]
    for array in own:
        for s in range(2, spans, 2):
            far = permute(array, "tm", [(i, i + s) for i in range(spans - s)])
            groups[s].append(far)
            groups[s + 1].append(permute(far, "tm", swap))
        groups[1].append(permute(array, "tm", swap_up))
    flags = jnp.stack(flags)
    seen_spans = list(enumerate(groups))

    columns = out_weight.shape[1]
    width = columns // COL_BLOCKS
    project = lambda a, j: jnp.dot(
        a, out_weight[:, j * width : (j + 1) * width], preferred_element_type=jnp.float32
    ).astype(jnp.bfloat16)
    returned = [[] for _ in range(COL_BLOCKS)]
    q_own = q_parts[0]
    for d in range(1, splits):
        attended = attend(q_parts[d], seen_spans, flags)
        for j in range(COL_BLOCKS):
            back = [((i + d) % splits, i) for i in range(splits)]
            returned[j].append(permute(project(attended, j), "head", back))
        q_own, attended = lax.optimization_barrier((q_own, attended))
    attended = attend(q_own, seen_spans, flags)
    level_now = lax.dynamic_index_in_dim(levels, span, 0, keepdims=False)
    gate_row = lax.dynamic_index_in_dim(gates, level_now, 0, keepdims=False)
    outs = []
    for j in range(COL_BLOCKS):
        cols = slice(j * width, (j + 1) * width)
        total = project(attended, j).astype(jnp.float32)
        for a in returned[j]:
            total = total + a.astype(jnp.float32)
        outs.append(
            (hidden[:, cols].astype(jnp.float32) + gate_row[None, cols] * total).astype(jnp.bfloat16)
        )
    return jnp.concatenate(outs, axis=1)


def solution(mesh):
    sizes = (mesh.shape["tm"], mesh.shape["head"], mesh.shape["branch"])
    return jax.shard_map(
        functools.partial(body, sizes),
        mesh=mesh,
        in_specs=(
            P("branch", "tm", "head", None, None),
            P("branch", "tm", "head", None, None),
            P("branch", "tm", "head", None, None),
            P("tm", ("head", "branch"), None, None),
            P("tm", ("head", "branch"), None, None),
            P("branch", "tm", "head", None),
            P("head", None),
            P(),
            P(),
            P(),
            P(),
        ),
        out_specs=P("branch", "tm", "head", None),
        check_vma=False,
    )
```

```python
import functools
import math

import jax
import jax.numpy as jnp
from jax import lax
from jax.experimental import pallas as pl
from jax.experimental.pallas import tpu as pltpu
from jax.sharding import PartitionSpec as P

NEG_BIG = -1e30
LOG2E = 1.4426950408889634
COL_BLOCKS = 8
HEAD_STEP_SCORES = 3 << 20
VMEM_LIMIT = 22 << 20


def flash_kernel(flags, *refs, layout, scale, step, first, last):
    count = sum(len(members) for _, members in layout)
    q_ref, kv_refs, refs = refs[0], refs[1 : 1 + count], refs[1 + count :]
    if not first:
        (max_in, sum_in, acc_in), refs = refs[:3], refs[3:]
    outs, score_ref = refs[:-1], refs[-1]
    dim = q_ref.shape[2]
    order = [(flag, i) for flag, members in layout for i in members]
    for h in range(step):
        block = jnp.concatenate([kv_refs[i][0, h] for _, i in order], axis=0)
        raw = lax.dot_general(
            q_ref[h], block, (((1,), (1,)), ((), ())), preferred_element_type=jnp.float32
        )
        at, top = 0, None
        for flag, i in order:
            bias = jnp.where(flags[flag] > 0, 0.0, NEG_BIG)
            for _ in range(0, kv_refs[i].shape[2], dim):
                piece = raw[:, at : at + dim] + bias
                score_ref[h, :, at : at + dim] = piece
                top = piece if top is None else jnp.maximum(top, piece)
                at += dim
        top = jnp.broadcast_to(jnp.max(top, axis=1, keepdims=True) * scale, top.shape)
        total = acc = None
        if not first:
            old = max_in[h]
            top = jnp.maximum(top, old)
            shrink = jnp.exp2(old - top)
            total, acc = sum_in[h] * shrink, acc_in[h] * shrink
        weights = []
        for j in range(0, at, dim):
            piece = jnp.exp2(score_ref[h, :, j : j + dim] * scale - top)
            total = piece if total is None else total + piece
            weights.append(piece.astype(jnp.bfloat16))
        block = jnp.concatenate([kv_refs[i][1, h] for _, i in order], axis=0)
        added = jnp.dot(
            jnp.concatenate(weights, axis=1), block, preferred_element_type=jnp.float32
        )
        acc = added if acc is None else acc + added
        if last:
            total = jnp.sum(total, axis=1, keepdims=True)
            outs[0][:, h * dim : (h + 1) * dim] = (acc / total).astype(outs[0].dtype)
        else:
            outs[0][h], outs[1][h], outs[2][h] = top, total, acc


def attend(queries, spans, flags, state, last):
    heads, rows, dim = queries.shape
    arrays, layout = [], []
    for flag, members in spans:
        layout.append((flag, tuple(range(len(arrays), len(arrays) + len(members)))))
        arrays += members
    keys = sum(array.shape[2] for array in arrays)
    step = max(s for s in range(1, heads + 1) if heads % s == 0 and s * rows * keys <= HEAD_STEP_SCORES)
    by_head = pl.BlockSpec((step, rows, dim), lambda h, f: (h, 0, 0))
    states = [] if state is None else list(state)
    return pl.pallas_call(
        functools.partial(
            flash_kernel,
            layout=tuple(layout),
            scale=LOG2E / math.sqrt(dim),
            step=step,
            first=state is None,
            last=last,
        ),
        out_shape=jax.ShapeDtypeStruct((rows, heads * dim), jnp.bfloat16)
        if last
        else [jax.ShapeDtypeStruct((heads, rows, dim), jnp.float32)] * 3,
        grid_spec=pltpu.PrefetchScalarGridSpec(
            num_scalar_prefetch=1,
            grid=(heads // step,),
            in_specs=[by_head]
            + [
                pl.BlockSpec((2, step, array.shape[2], dim), lambda h, f: (0, h, 0, 0))
                for array in arrays
            ]
            + [by_head] * len(states),
            out_specs=pl.BlockSpec((rows, step * dim), lambda h, f: (0, h)) if last else [by_head] * 3,
            scratch_shapes=[pltpu.VMEM((step, rows, keys), jnp.float32)],
        ),
        cost_estimate=pl.CostEstimate(
            flops=4 * heads * rows * keys * dim,
            bytes_accessed=2 * heads * dim * (2 * rows + 2 * keys),
            transcendentals=heads * rows * keys,
        ),
        compiler_params=pltpu.CompilerParams(vmem_limit_bytes=VMEM_LIMIT),
    )(flags, queries, *arrays, *states)


def body(sizes, queries, keys, values, ctx_keys, ctx_values, hidden, out_weight, gates, levels, span_mask, prefix):
    return sublayer(
        sizes, queries[0, 0], keys[0, 0], values[0, 0], ctx_keys[0], ctx_values[0], hidden[0, 0],
        out_weight, gates, levels, span_mask, prefix,
    )[None, None]


def sublayer(sizes, queries, keys, values, ctx_keys, ctx_values, hidden, out_weight, gates, levels, span_mask, prefix):
    spans, splits, branches = sizes
    span = lax.axis_index("tm")
    part = lax.axis_index("head")
    branch = lax.axis_index("branch")
    to_heads = lambda a: jnp.transpose(a, (1, 0, 2))
    q, k, v = to_heads(queries), to_heads(keys), to_heads(values)
    ck, cv = to_heads(ctx_keys), to_heads(ctx_values)
    group = q.shape[0] // splits
    take = lambda a, d: lax.dynamic_slice_in_dim(a, lax.rem(part + d, splits) * group, group, 0)
    pair = lambda a, b, d: jnp.stack([take(a, d), take(b, d)])
    cycle = lambda d: [(i, (i + d) % splits) for i in range(splits)]

    swap_up = [(i, i + 1) for i in range(0, spans, 2)]
    swap = swap_up + [(i + 1, i) for i in range(0, spans, 2)]
    mask_row = lax.dynamic_index_in_dim(span_mask, span, 0, keepdims=False)
    ids = jnp.arange(spans, dtype=jnp.int32)
    seen = lambda s: jnp.sum(jnp.where((ids == s) & (ids <= span), mask_row, 0))
    partner = span + 1 - 2 * lax.rem(span, 2)
    flags = [jnp.int32(1), seen(partner)]
    for s in range(2, spans, 2):
        flags += [seen(span - s), seen(partner - s)]
    flags = jnp.stack(flags)
    level_now = lax.dynamic_index_in_dim(levels, span, 0, keepdims=False)
    gate_row = lax.dynamic_index_in_dim(gates, level_now, 0, keepdims=False)

    ctx_parts, kv_parts, q_parts = [pair(ck, cv, 0)], [pair(k, v, 0)], [take(q, 0)]
    for d in range(1, splits):
        ctx_parts.append(lax.ppermute(pair(ck, cv, d), "head", cycle(d)))
    for d in range(1, splits):
        kv_parts.append(lax.ppermute(pair(k, v, d), "head", cycle(d)))
    for d in range(1, splits):
        q_parts.append(lax.ppermute(take(q, d), "head", cycle(d)))

    use_context = span < prefix[0]
    first = jnp.concatenate(ctx_parts, axis=2)
    piece_rows, rows = first.shape[2], k.shape[1]
    up, down, own, held = [first], [first], [], []
    for s in range(branches):
        piece = first
        if s > 0:
            if s == 2:
                up[-1], flags, gate_row = lax.optimization_barrier((up[-1], flags, gate_row))
            up.append(lax.ppermute(up[-1], "branch", [(i, i + 1) for i in range(s - 1, branches - 1)]))
            down.append(lax.ppermute(down[-1], "branch", [(i, i - 1) for i in range(1, branches - s + 1)]))
            held[-1], piece = lax.optimization_barrier((own[-1], up[s]))
            for t in range(1, s + 1):
                piece = jnp.where(branch == s - t, down[t], piece)
        d, at = divmod(s * piece_rows, rows)
        own.append(jnp.where(use_context, piece, kv_parts[d][:, :, at : at + piece_rows]))
        held.append(own[-1])

    groups = [held, []]
    for _ in range(2, spans, 2):
        groups += [[], []]
    for array in own:
        for s in range(2, spans, 2):
            far = lax.ppermute(array, "tm", [(i, i + s) for i in range(spans - s)])
            groups[s].append(far)
            groups[s + 1].append(lax.ppermute(far, "tm", swap))
        groups[1].append(lax.ppermute(array, "tm", swap_up))

    half = max(1, len(own) // 2)
    early = [(i, arrays[:half]) for i, arrays in enumerate(groups)]
    late = [(i, arrays[half:]) for i, arrays in enumerate(groups)]
    states = []
    for d in range(splits):
        states.append(attend(q_parts[d], early, flags, None, False))

    columns = out_weight.shape[1]
    width = columns // COL_BLOCKS
    project = lambda a, w: jnp.dot(a, w, preferred_element_type=jnp.float32).astype(jnp.bfloat16)
    returned = [[] for _ in range(COL_BLOCKS)]
    for d in range(1, splits):
        attended = attend(q_parts[d], late, flags, states[d], True)
        back = [((i + d) % splits, i) for i in range(splits)]
        for j in range(COL_BLOCKS):
            partial = project(attended, out_weight[:, j * width : (j + 1) * width])
            returned[j].append(lax.ppermute(partial, "head", back))
    attended = attend(q_parts[0], late, flags, states[0], True)
    kept = lax.optimization_barrier(project(attended, out_weight))
    updated = hidden
    for j in range(COL_BLOCKS):
        cols = slice(j * width, (j + 1) * width)
        total = kept[:, cols].astype(jnp.float32)
        for a in returned[j]:
            total = total + a.astype(jnp.float32)
        fresh = updated[:, cols].astype(jnp.float32) + gate_row[None, cols] * total
        updated = lax.dynamic_update_slice_in_dim(updated, fresh.astype(jnp.bfloat16), j * width, 1)
    return updated


def solution(mesh):
    sizes = (mesh.shape["tm"], mesh.shape["head"], mesh.shape["branch"])
    return jax.shard_map(
        functools.partial(body, sizes),
        mesh=mesh,
        in_specs=(
            P("branch", "tm", "head", None, None),
            P("branch", "tm", "head", None, None),
            P("branch", "tm", "head", None, None),
            P("tm", ("head", "branch"), None, None),
            P("tm", ("head", "branch"), None, None),
            P("branch", "tm", "head", None),
            P("head", None),
            P(),
            P(),
            P(),
            P(),
        ),
        out_specs=P("branch", "tm", "head", None),
        check_vma=False,
    )
```

```python
import functools
import math

import jax
import jax.numpy as jnp
from jax import lax
from jax.experimental import pallas as pl
from jax.experimental.pallas import tpu as pltpu
from jax.sharding import PartitionSpec as P

NEG_BIG = -1e30
LOG2E = 1.4426950408889634
COL_BLOCKS = 5
HEAD_STEP_SCORES = 3 << 20
VMEM_LIMIT = 22 << 20


def flash_kernel(flags, *refs, layout, scale, step, first, last):
    count = sum(len(members) for _, members in layout)
    q_ref, kv_refs, refs = refs[0], refs[1 : 1 + count], refs[1 + count :]
    if not first:
        (max_in, sum_in, acc_in), refs = refs[:3], refs[3:]
    outs, score_ref = refs[:-1], refs[-1]
    dim = q_ref.shape[2]
    order = [(flag, i) for flag, members in layout for i in members]
    for h in range(step):
        block = jnp.concatenate([kv_refs[i][0, h] for _, i in order], axis=0)
        raw = lax.dot_general(
            q_ref[h], block, (((1,), (1,)), ((), ())), preferred_element_type=jnp.float32
        )
        at, top = 0, None
        for flag, i in order:
            bias = jnp.where(flags[flag] > 0, 0.0, NEG_BIG)
            for _ in range(0, kv_refs[i].shape[2], dim):
                piece = raw[:, at : at + dim] + bias
                score_ref[h, :, at : at + dim] = piece
                top = piece if top is None else jnp.maximum(top, piece)
                at += dim
        top = jnp.broadcast_to(jnp.max(top, axis=1, keepdims=True) * scale, top.shape)
        total = acc = None
        if not first:
            old = max_in[h]
            top = jnp.maximum(top, old)
            shrink = jnp.exp2(old - top)
            total, acc = sum_in[h] * shrink, acc_in[h] * shrink
        weights = []
        for j in range(0, at, dim):
            piece = jnp.exp2(score_ref[h, :, j : j + dim] * scale - top)
            total = piece if total is None else total + piece
            weights.append(piece.astype(jnp.bfloat16))
        block = jnp.concatenate([kv_refs[i][1, h] for _, i in order], axis=0)
        added = jnp.dot(
            jnp.concatenate(weights, axis=1), block, preferred_element_type=jnp.float32
        )
        acc = added if acc is None else acc + added
        if last:
            total = jnp.sum(total, axis=1, keepdims=True)
            outs[0][:, h * dim : (h + 1) * dim] = (acc / total).astype(outs[0].dtype)
        else:
            outs[0][h], outs[1][h], outs[2][h] = top, total, acc


def attend(queries, spans, flags, state, last):
    heads, rows, dim = queries.shape
    arrays, layout = [], []
    for flag, members in spans:
        layout.append((flag, tuple(range(len(arrays), len(arrays) + len(members)))))
        arrays += members
    keys = sum(array.shape[2] for array in arrays)
    step = max(s for s in range(1, heads + 1) if heads % s == 0 and s * rows * keys <= HEAD_STEP_SCORES)
    by_head = pl.BlockSpec((step, rows, dim), lambda h, f: (h, 0, 0))
    states = [] if state is None else list(state)
    return pl.pallas_call(
        functools.partial(
            flash_kernel,
            layout=tuple(layout),
            scale=LOG2E / math.sqrt(dim),
            step=step,
            first=state is None,
            last=last,
        ),
        out_shape=jax.ShapeDtypeStruct((rows, heads * dim), jnp.bfloat16)
        if last
        else [jax.ShapeDtypeStruct((heads, rows, dim), jnp.float32)] * 3,
        grid_spec=pltpu.PrefetchScalarGridSpec(
            num_scalar_prefetch=1,
            grid=(heads // step,),
            in_specs=[by_head]
            + [
                pl.BlockSpec((2, step, array.shape[2], dim), lambda h, f: (0, h, 0, 0))
                for array in arrays
            ]
            + [by_head] * len(states),
            out_specs=pl.BlockSpec((rows, step * dim), lambda h, f: (0, h)) if last else [by_head] * 3,
            scratch_shapes=[pltpu.VMEM((step, rows, keys), jnp.float32)],
        ),
        cost_estimate=pl.CostEstimate(
            flops=4 * heads * rows * keys * dim,
            bytes_accessed=2 * heads * dim * (2 * rows + 2 * keys),
            transcendentals=heads * rows * keys,
        ),
        compiler_params=pltpu.CompilerParams(vmem_limit_bytes=VMEM_LIMIT),
    )(flags, queries, *arrays, *states)


def body(sizes, queries, keys, values, ctx_keys, ctx_values, hidden, out_weight, gates, levels, span_mask, prefix):
    return sublayer(
        sizes, queries[0, 0], keys[0, 0], values[0, 0], ctx_keys[0], ctx_values[0], hidden[0, 0],
        out_weight, gates, levels, span_mask, prefix,
    )[None, None]


def sublayer(sizes, queries, keys, values, ctx_keys, ctx_values, hidden, out_weight, gates, levels, span_mask, prefix):
    spans, splits, branches = sizes
    span = lax.axis_index("tm")
    part = lax.axis_index("head")
    branch = lax.axis_index("branch")
    to_heads = lambda a: jnp.transpose(a, (1, 0, 2))
    q, k, v = to_heads(queries), to_heads(keys), to_heads(values)
    ck, cv = to_heads(ctx_keys), to_heads(ctx_values)
    group = q.shape[0] // splits
    take = lambda a, d: lax.dynamic_slice_in_dim(a, lax.rem(part + d, splits) * group, group, 0)
    pair = lambda a, b, d: jnp.stack([take(a, d), take(b, d)])
    cycle = lambda d: [(i, (i + d) % splits) for i in range(splits)]

    swap_up = [(i, i + 1) for i in range(0, spans, 2)]
    swap = swap_up + [(i + 1, i) for i in range(0, spans, 2)]
    mask_row = lax.dynamic_index_in_dim(span_mask, span, 0, keepdims=False)
    ids = jnp.arange(spans, dtype=jnp.int32)
    seen = lambda s: jnp.sum(jnp.where((ids == s) & (ids <= span), mask_row, 0))
    partner = span + 1 - 2 * lax.rem(span, 2)
    flags = [jnp.int32(1), seen(partner)]
    for s in range(2, spans, 2):
        flags += [seen(span - s), seen(partner - s)]
    flags = jnp.stack(flags)
    level_now = lax.dynamic_index_in_dim(levels, span, 0, keepdims=False)
    gate_row = lax.dynamic_index_in_dim(gates, level_now, 0, keepdims=False)

    ctx_parts, kv_parts, q_parts = [pair(ck, cv, 0)], [pair(k, v, 0)], [take(q, 0)]
    for d in range(1, splits):
        ctx_parts.append(lax.ppermute(pair(ck, cv, d), "head", cycle(d)))
    for d in range(1, splits):
        kv_parts.append(lax.ppermute(pair(k, v, d), "head", cycle(d)))
    for d in range(1, splits):
        q_parts.append(lax.ppermute(take(q, d), "head", cycle(d)))

    use_context = span < prefix[0]
    up, down = [[a] for a in ctx_parts], [[a] for a in ctx_parts]
    piece_rows, rows = splits * ctx_parts[0].shape[2], k.shape[1]
    own, held = [], []
    for s in range(branches):
        pieces = []
        for d in range(splits):
            piece = ctx_parts[d]
            if s > 0:
                if s == branches - 1 and d == 0:
                    up[0][-1], flags, gate_row = lax.optimization_barrier((up[0][-1], flags, gate_row))
                rise = [(i, i + 1) for i in range(s - 1, branches - 1)]
                fall = [(i, i - 1) for i in range(1, branches - s + 1)]
                up[d].append(lax.ppermute(up[d][-1], "branch", rise))
                down[d].append(lax.ppermute(down[d][-1], "branch", fall))
                piece = up[d][s]
            pieces.append(piece)
        if s > 0:
            held[-1], *pieces = lax.optimization_barrier((own[-1], *pieces))
            for d in range(splits):
                for t in range(1, s + 1):
                    pieces[d] = jnp.where(branch == s - t, down[d][t], pieces[d])
        d, at = divmod(s * piece_rows, rows)
        context = jnp.concatenate(pieces, axis=2)
        own.append(jnp.where(use_context, context, kv_parts[d][:, :, at : at + piece_rows]))
        held.append(own[-1])

    groups = [held, []]
    for _ in range(2, spans, 2):
        groups += [[], []]
    for array in own:
        for s in range(2, spans, 2):
            far = lax.ppermute(array, "tm", [(i, i + s) for i in range(spans - s)])
            groups[s].append(far)
            groups[s + 1].append(lax.ppermute(far, "tm", swap))
        groups[1].append(lax.ppermute(array, "tm", swap_up))

    half = max(1, len(own) // 2)
    early = [(i, arrays[:half]) for i, arrays in enumerate(groups)]
    late = [(i, arrays[half:]) for i, arrays in enumerate(groups)]
    states = []
    for d in range(splits):
        states.append(attend(q_parts[d], early, flags, None, False))

    columns = out_weight.shape[1]
    width = columns // COL_BLOCKS
    project = lambda a, w: jnp.dot(a, w, preferred_element_type=jnp.float32).astype(jnp.bfloat16)
    returned = [[] for _ in range(COL_BLOCKS)]
    for d in range(1, splits):
        attended = attend(q_parts[d], late, flags, states[d], True)
        back = [((i + d) % splits, i) for i in range(splits)]
        for j in range(COL_BLOCKS):
            partial = project(attended, out_weight[:, j * width : (j + 1) * width])
            returned[j].append(lax.ppermute(partial, "head", back))
    attended = attend(q_parts[0], late, flags, states[0], True)
    kept = lax.optimization_barrier(project(attended, out_weight))
    updated = hidden
    for j in range(COL_BLOCKS):
        cols = slice(j * width, (j + 1) * width)
        total = kept[:, cols].astype(jnp.float32)
        for a in returned[j]:
            total = total + a.astype(jnp.float32)
        fresh = updated[:, cols].astype(jnp.float32) + gate_row[None, cols] * total
        updated = lax.dynamic_update_slice_in_dim(updated, fresh.astype(jnp.bfloat16), j * width, 1)
    return updated


def solution(mesh):
    sizes = (mesh.shape["tm"], mesh.shape["head"], mesh.shape["branch"])
    return jax.shard_map(
        functools.partial(body, sizes),
        mesh=mesh,
        in_specs=(
            P("branch", "tm", "head", None, None),
            P("branch", "tm", "head", None, None),
            P("branch", "tm", "head", None, None),
            P("tm", ("head", "branch"), None, None),
            P("tm", ("head", "branch"), None, None),
            P("branch", "tm", "head", None),
            P("head", None),
            P(),
            P(),
            P(),
            P(),
        ),
        out_specs=P("branch", "tm", "head", None),
        check_vma=False,
    )
```

```python
import functools
import math

import jax
import jax.numpy as jnp
from jax import lax
from jax.experimental import pallas as pl
from jax.experimental.pallas import tpu as pltpu
from jax.sharding import PartitionSpec as P

NEG_BIG = -1e30
LOG2E = 1.4426950408889634
COL_BLOCKS = 5
HEAD_STEP_SCORES = 3 << 20
VMEM_LIMIT = 22 << 20


def hidden_bias(mask, span, origin):
    source = origin(span)
    return jnp.where((source >= 0) & (mask[span, jnp.maximum(source, 0)] > 0), 0.0, NEG_BIG)


def flash_kernel(mask, *refs, layout, count, scale, step, first, last):
    q_ref, kv_refs, refs = refs[0], refs[1 : 1 + count], refs[1 + count :]
    span = lax.axis_index("tm")
    odd = lax.rem(span, 2) == 1
    biases = [None if origin is None else hidden_bias(mask, span, origin) for origin, _ in layout]

    def gather(kind, h):
        blocks = []
        for _, members in layout:
            for i in members:
                if isinstance(i, tuple):
                    blocks.append(jnp.where(odd, kv_refs[i[0]][kind, h], kv_refs[i[1]][kind, h]))
                else:
                    blocks.append(kv_refs[i][kind, h])
        return jnp.concatenate(blocks, axis=0)

    if not first:
        (max_in, sum_in, acc_in), refs = refs[:3], refs[3:]
    outs, score_ref = refs[:-1], refs[-1]
    dim = q_ref.shape[2]
    keys = kv_refs[0].shape[2]
    order = [bias for bias, (_, members) in zip(biases, layout) for _ in members]
    for h in range(step):
        raw = lax.dot_general(
            q_ref[h], gather(0, h), (((1,), (1,)), ((), ())), preferred_element_type=jnp.float32
        )
        at, top = 0, None
        for bias in order:
            for _ in range(0, keys, dim):
                piece = raw[:, at : at + dim]
                if bias is not None:
                    piece = piece + bias
                score_ref[h, :, at : at + dim] = piece
                top = piece if top is None else jnp.maximum(top, piece)
                at += dim
        top = jnp.broadcast_to(jnp.max(top, axis=1, keepdims=True) * scale, top.shape)
        total = acc = None
        if not first:
            old = max_in[h]
            top = jnp.maximum(top, old)
            shrink = jnp.exp2(old - top)
            total, acc = sum_in[h] * shrink, acc_in[h] * shrink
        weights = []
        for j in range(0, at, dim):
            piece = jnp.exp2(score_ref[h, :, j : j + dim] * scale - top)
            total = piece if total is None else total + piece
            weights.append(piece.astype(jnp.bfloat16))
        added = jnp.dot(
            jnp.concatenate(weights, axis=1), gather(1, h), preferred_element_type=jnp.float32
        )
        acc = added if acc is None else acc + added
        if last:
            total = jnp.sum(total, axis=1, keepdims=True)
            outs[0][:, h * dim : (h + 1) * dim] = (acc / total).astype(outs[0].dtype)
        else:
            outs[0][h], outs[1][h], outs[2][h] = top, total, acc


def attend(queries, slots, span_mask, state, last):
    heads, rows, dim = queries.shape
    arrays, layout = [], []
    for origin, members in slots:
        places = []
        for member in members:
            choices = member if isinstance(member, tuple) else (member,)
            at = tuple(range(len(arrays), len(arrays) + len(choices)))
            places.append(at if len(at) > 1 else at[0])
            arrays += choices
        layout.append((origin, places))
    keys = arrays[0].shape[2] * sum(len(places) for _, places in layout)
    step = max(s for s in range(1, heads + 1) if heads % s == 0 and s * rows * keys <= HEAD_STEP_SCORES)
    by_head = pl.BlockSpec((step, rows, dim), lambda h, f: (h, 0, 0))
    states = [] if state is None else list(state)
    return pl.pallas_call(
        functools.partial(
            flash_kernel,
            layout=layout,
            count=len(arrays),
            scale=LOG2E / math.sqrt(dim),
            step=step,
            first=state is None,
            last=last,
        ),
        out_shape=jax.ShapeDtypeStruct((rows, heads * dim), jnp.bfloat16)
        if last
        else [jax.ShapeDtypeStruct((heads, rows, dim), jnp.float32)] * 3,
        grid_spec=pltpu.PrefetchScalarGridSpec(
            num_scalar_prefetch=1,
            grid=(heads // step,),
            in_specs=[by_head]
            + [
                pl.BlockSpec((2, step, array.shape[2], dim), lambda h, f: (0, h, 0, 0))
                for array in arrays
            ]
            + [by_head] * len(states),
            out_specs=pl.BlockSpec((rows, step * dim), lambda h, f: (0, h)) if last else [by_head] * 3,
            scratch_shapes=[pltpu.VMEM((step, rows, keys), jnp.float32)],
        ),
        cost_estimate=pl.CostEstimate(
            flops=4 * heads * rows * keys * dim,
            bytes_accessed=2 * heads * dim * (2 * rows + 2 * keys),
            transcendentals=heads * rows * keys,
        ),
        compiler_params=pltpu.CompilerParams(vmem_limit_bytes=VMEM_LIMIT),
    )(span_mask, queries, *arrays, *states)


def body(sizes, queries, keys, values, ctx_keys, ctx_values, hidden, out_weight, gates, levels, span_mask, prefix):
    return sublayer(
        sizes, queries[0, 0], keys[0, 0], values[0, 0], ctx_keys[0], ctx_values[0], hidden[0, 0],
        out_weight, gates, levels, span_mask, prefix,
    )[None, None]


def sublayer(sizes, queries, keys, values, ctx_keys, ctx_values, hidden, out_weight, gates, levels, span_mask, prefix):
    spans, splits, branches = sizes
    span = lax.axis_index("tm")
    part = lax.axis_index("head")
    branch = lax.axis_index("branch")
    to_heads = lambda a: jnp.transpose(a, (1, 0, 2))
    q, k, v = to_heads(queries), to_heads(keys), to_heads(values)
    ck, cv = to_heads(ctx_keys), to_heads(ctx_values)
    group = q.shape[0] // splits
    take = lambda a, d: lax.dynamic_slice_in_dim(a, lax.rem(part + d, splits) * group, group, 0)
    pair = lambda a, b, d: jnp.stack([take(a, d), take(b, d)])
    cycle = lambda d: [(i, (i + d) % splits) for i in range(splits)]

    level_now = lax.dynamic_index_in_dim(levels, span, 0, keepdims=False)
    gate_row = lax.dynamic_index_in_dim(gates, level_now, 0, keepdims=False)

    ctx_parts, kv_parts, q_parts = [pair(ck, cv, 0)], [pair(k, v, 0)], [take(q, 0)]
    for d in range(1, splits):
        ctx_parts.append(lax.ppermute(pair(ck, cv, d), "head", cycle(d)))
    for d in range(1, splits):
        kv_parts.append(lax.ppermute(pair(k, v, d), "head", cycle(d)))
    for d in range(1, splits):
        q_parts.append(lax.ppermute(take(q, d), "head", cycle(d)))

    use_context = span < prefix[0]
    final = spans - 1
    stands_in = span == final
    bases = [jnp.where(stands_in, lax.ppermute(a, "tm", [(0, final)]), a) for a in ctx_parts]
    up, down = [[a] for a in bases], [[a] for a in bases]
    piece_rows, rows = splits * bases[0].shape[2], k.shape[1]
    own, passed, held = [], [], []
    for s in range(branches):
        pieces = []
        for d in range(splits):
            piece = bases[d]
            if s > 0:
                if s == branches - 1 and d == 0:
                    up[0][-1], gate_row = lax.optimization_barrier((up[0][-1], gate_row))
                rise = [(i, i + 1) for i in range(s - 1, branches - 1)]
                fall = [(i, i - 1) for i in range(1, branches - s + 1)]
                up[d].append(lax.ppermute(up[d][-1], "branch", rise))
                down[d].append(lax.ppermute(down[d][-1], "branch", fall))
                piece = up[d][s]
            pieces.append(piece)
        if s > 0:
            merged, *pieces = lax.optimization_barrier(((own[-1], passed[-1]), *pieces))
            held[-1] = merged
            for d in range(splits):
                for t in range(1, s + 1):
                    pieces[d] = jnp.where(branch == s - t, down[d][t], pieces[d])
        d, at = divmod(s * piece_rows, rows)
        context, mine = jnp.concatenate(pieces, axis=2), kv_parts[d][:, :, at : at + piece_rows]
        own.append(jnp.where(use_context, context, mine))
        passed.append(jnp.where(use_context | stands_in, context, mine))
        held.append((own[-1], passed[-1]))

    pairs = [(i, i + 1) for i in range(0, spans, 2)]
    beside = [lax.ppermute(a, "tm", pairs + [(final, final - 1)]) for a in passed]
    slots = [
        (None, [a for a, _ in held]),
        (lambda c: jnp.where(lax.rem(c, 2) == 1, c - 1, jnp.where(c == final - 1, 0, -1)), beside),
    ]
    for s in range(2, final - 1, 2):
        far = [lax.ppermute(a, "tm", [(i, i + s) for i in range(spans - s)]) for a in own]
        back = [(b, a) for a, b in pairs]
        near = [lax.ppermute(a, "tm", pairs + back) for a in far]
        slots.append((lambda c, s=s: c - s, far))
        slots.append((lambda c, s=s: c + 1 - 2 * lax.rem(c, 2) - s, near))
    s = final - 1
    far = [lax.ppermute(a, "tm", [(1, final)]) for a in own]
    near = [lax.ppermute(a, "tm", [(final, final - 1)]) for a in far]
    slots.append((lambda c: jnp.where(c >= final - 1, 1, -1), list(zip(far, near))))
    slots.append((lambda c: jnp.where(c == final, 0, -1), [a for _, a in held]))

    half = max(1, len(own) // 2)
    early = [(origin, arrays[:half]) for origin, arrays in slots]
    late = [(origin, arrays[half:]) for origin, arrays in slots]
    states = []
    for d in range(splits):
        states.append(attend(q_parts[d], early, span_mask, None, False))

    columns = out_weight.shape[1]
    width = columns // COL_BLOCKS
    project = lambda a, w: jnp.dot(a, w, preferred_element_type=jnp.float32).astype(jnp.bfloat16)
    returned = [[] for _ in range(COL_BLOCKS)]
    for d in range(1, splits):
        attended = attend(q_parts[d], late, span_mask, states[d], True)
        back = [((i + d) % splits, i) for i in range(splits)]
        for j in range(COL_BLOCKS):
            partial = project(attended, out_weight[:, j * width : (j + 1) * width])
            returned[j].append(lax.ppermute(partial, "head", back))
    attended = attend(q_parts[0], late, span_mask, states[0], True)
    kept = lax.optimization_barrier(project(attended, out_weight))
    updated = hidden
    for j in range(COL_BLOCKS):
        cols = slice(j * width, (j + 1) * width)
        total = kept[:, cols].astype(jnp.float32)
        for a in returned[j]:
            total = total + a.astype(jnp.float32)
        fresh = updated[:, cols].astype(jnp.float32) + gate_row[None, cols] * total
        updated = lax.dynamic_update_slice_in_dim(updated, fresh.astype(jnp.bfloat16), j * width, 1)
    return updated


def solution(mesh):
    sizes = (mesh.shape["tm"], mesh.shape["head"], mesh.shape["branch"])
    return jax.shard_map(
        functools.partial(body, sizes),
        mesh=mesh,
        in_specs=(
            P("branch", "tm", "head", None, None),
            P("branch", "tm", "head", None, None),
            P("branch", "tm", "head", None, None),
            P("tm", ("head", "branch"), None, None),
            P("tm", ("head", "branch"), None, None),
            P("branch", "tm", "head", None),
            P("head", None),
            P(),
            P(),
            P(),
            P(),
        ),
        out_specs=P("branch", "tm", "head", None),
        check_vma=False,
    )
```

```python
import functools
import math

import jax
import jax.numpy as jnp
from jax import lax
from jax.experimental import pallas as pl
from jax.experimental.pallas import tpu as pltpu
from jax.sharding import PartitionSpec as P

NEG_BIG = -1e30
LOG2E = 1.4426950408889634
COL_BLOCKS = 5
HEAD_STEP_SCORES = 3 << 20
VMEM_LIMIT = 22 << 20


def hidden_bias(mask, span, origin):
    source = origin(span)
    return jnp.where((source >= 0) & (mask[span, jnp.maximum(source, 0)] > 0), 0.0, NEG_BIG)


def flash_kernel(mask, *refs, layout, count, scale, step, first, last):
    q_ref, kv_refs, refs = refs[0], refs[1 : 1 + count], refs[1 + count :]
    span = lax.axis_index("tm")
    odd = lax.rem(span, 2) == 1
    biases = [None if origin is None else hidden_bias(mask, span, origin) for origin, _ in layout]

    def gather(kind, h):
        blocks = []
        for _, members in layout:
            for i in members:
                if isinstance(i, tuple):
                    blocks.append(jnp.where(odd, kv_refs[i[0]][kind, h], kv_refs[i[1]][kind, h]))
                else:
                    blocks.append(kv_refs[i][kind, h])
        return jnp.concatenate(blocks, axis=0)

    if not first:
        (max_in, sum_in, acc_in), refs = refs[:3], refs[3:]
    outs, score_ref = refs[:-1], refs[-1]
    dim = q_ref.shape[2]
    keys = kv_refs[0].shape[2]
    order = [bias for bias, (_, members) in zip(biases, layout) for _ in members]
    for h in range(step):
        raw = lax.dot_general(
            q_ref[h], gather(0, h), (((1,), (1,)), ((), ())), preferred_element_type=jnp.float32
        )
        at, top = 0, None
        for bias in order:
            for _ in range(0, keys, dim):
                piece = raw[:, at : at + dim]
                if bias is not None:
                    piece = piece + bias
                score_ref[h, :, at : at + dim] = piece
                top = piece if top is None else jnp.maximum(top, piece)
                at += dim
        top = jnp.broadcast_to(jnp.max(top, axis=1, keepdims=True) * scale, top.shape)
        total = acc = None
        if not first:
            old = max_in[h]
            top = jnp.maximum(top, old)
            shrink = jnp.exp2(old - top)
            total, acc = sum_in[h] * shrink, acc_in[h] * shrink
        weights = []
        for j in range(0, at, dim):
            piece = jnp.exp2(score_ref[h, :, j : j + dim] * scale - top)
            total = piece if total is None else total + piece
            weights.append(piece.astype(jnp.bfloat16))
        added = jnp.dot(
            jnp.concatenate(weights, axis=1), gather(1, h), preferred_element_type=jnp.float32
        )
        acc = added if acc is None else acc + added
        if last:
            total = jnp.sum(total, axis=1, keepdims=True)
            outs[0][:, h * dim : (h + 1) * dim] = (acc / total).astype(outs[0].dtype)
        else:
            outs[0][h], outs[1][h], outs[2][h] = top, total, acc


def attend(queries, slots, span_mask, state, last):
    heads, rows, dim = queries.shape
    arrays, layout = [], []
    for origin, members in slots:
        places = []
        for member in members:
            choices = member if isinstance(member, tuple) else (member,)
            at = tuple(range(len(arrays), len(arrays) + len(choices)))
            places.append(at if len(at) > 1 else at[0])
            arrays += choices
        layout.append((origin, places))
    keys = arrays[0].shape[2] * sum(len(places) for _, places in layout)
    step = max(s for s in range(1, heads + 1) if heads % s == 0 and s * rows * keys <= HEAD_STEP_SCORES)
    by_head = pl.BlockSpec((step, rows, dim), lambda h, f: (h, 0, 0))
    states = [] if state is None else list(state)
    return pl.pallas_call(
        functools.partial(
            flash_kernel,
            layout=layout,
            count=len(arrays),
            scale=LOG2E / math.sqrt(dim),
            step=step,
            first=state is None,
            last=last,
        ),
        out_shape=jax.ShapeDtypeStruct((rows, heads * dim), jnp.bfloat16)
        if last
        else [jax.ShapeDtypeStruct((heads, rows, dim), jnp.float32)] * 3,
        grid_spec=pltpu.PrefetchScalarGridSpec(
            num_scalar_prefetch=1,
            grid=(heads // step,),
            in_specs=[by_head]
            + [
                pl.BlockSpec((2, step, array.shape[2], dim), lambda h, f: (0, h, 0, 0))
                for array in arrays
            ]
            + [by_head] * len(states),
            out_specs=pl.BlockSpec((rows, step * dim), lambda h, f: (0, h)) if last else [by_head] * 3,
            scratch_shapes=[pltpu.VMEM((step, rows, keys), jnp.float32)],
        ),
        cost_estimate=pl.CostEstimate(
            flops=4 * heads * rows * keys * dim,
            bytes_accessed=2 * heads * dim * (2 * rows + 2 * keys),
            transcendentals=heads * rows * keys,
        ),
        compiler_params=pltpu.CompilerParams(vmem_limit_bytes=VMEM_LIMIT),
    )(span_mask, queries, *arrays, *states)


def body(sizes, queries, keys, values, ctx_keys, ctx_values, hidden, out_weight, gates, levels, span_mask, prefix):
    return sublayer(
        sizes, queries[0, 0], keys[0, 0], values[0, 0], ctx_keys[0], ctx_values[0], hidden[0, 0],
        out_weight, gates, levels, span_mask, prefix,
    )[None, None]


def permute(array, axis, pairs):
    return lax.ppermute(array, axis, pairs)


def sublayer(sizes, queries, keys, values, ctx_keys, ctx_values, hidden, out_weight, gates, levels, span_mask, prefix):
    spans, splits, branches = sizes
    span = lax.axis_index("tm")
    part = lax.axis_index("head")
    to_heads = lambda a: jnp.transpose(a, (1, 0, 2))
    q, k, v = to_heads(queries), to_heads(keys), to_heads(values)
    ck, cv = to_heads(ctx_keys), to_heads(ctx_values)
    group = q.shape[0] // splits
    take = lambda a, d: lax.dynamic_slice_in_dim(a, lax.rem(part + d, splits) * group, group, 0)
    pair = lambda a, b, d: jnp.stack([take(a, d), take(b, d)])
    cycle = lambda d: [(i, (i + d) % splits) for i in range(splits)]

    level_now = lax.dynamic_index_in_dim(levels, span, 0, keepdims=False)
    gate_row = lax.dynamic_index_in_dim(gates, level_now, 0, keepdims=False)

    ctx_parts, kv_parts, q_parts = [pair(ck, cv, 0)], [pair(k, v, 0)], [take(q, 0)]
    for d in range(1, splits):
        ctx_parts.append(permute(pair(ck, cv, d), "head", cycle(d)))
    for d in range(1, splits):
        kv_parts.append(permute(pair(k, v, d), "head", cycle(d)))
    for d in range(1, splits):
        q_parts.append(permute(take(q, d), "head", cycle(d)))

    use_context = span < prefix[0]
    final = spans - 1
    stands_in = span == final
    first = jnp.concatenate(ctx_parts, axis=2)
    first = jnp.where(stands_in, permute(first, "tm", [(0, final)]), first)
    pieces, own, passed, held = [first], [], [], []
    piece_rows, rows = pieces[0].shape[2], k.shape[1]
    for i in range(1, branches):
        low = i & -i
        pieces.append(permute(pieces[i - low], "branch", [(b, b ^ low) for b in range(branches)]))
    for i, piece in enumerate(pieces):
        if own:
            held[-1], piece = lax.optimization_barrier(((own[-1], passed[-1]), piece))
        d, at = divmod(i * piece_rows, rows)
        mine = kv_parts[d][:, :, at : at + piece_rows]
        own.append(jnp.where(use_context, piece, mine))
        passed.append(jnp.where(use_context | stands_in, piece, mine))
        held.append((own[-1], passed[-1]))

    pairs = [(i, i + 1) for i in range(0, spans, 2)]
    beside = [permute(a, "tm", pairs + [(final, final - 1)]) for a in passed]
    slots = [
        (None, [a for a, _ in held]),
        (lambda c: jnp.where(lax.rem(c, 2) == 1, c - 1, jnp.where(c == final - 1, 0, -1)), beside),
    ]
    for s in range(2, final - 1, 2):
        far = [permute(a, "tm", [(i, i + s) for i in range(spans - s)]) for a in own]
        back = [(b, a) for a, b in pairs]
        near = [permute(a, "tm", pairs + back) for a in far]
        slots.append((lambda c, s=s: c - s, far))
        slots.append((lambda c, s=s: c + 1 - 2 * lax.rem(c, 2) - s, near))
    s = final - 1
    far = [permute(a, "tm", [(1, final)]) for a in own]
    near = [permute(a, "tm", [(final, final - 1)]) for a in far]
    slots.append((lambda c: jnp.where(c >= final - 1, 1, -1), list(zip(far, near))))
    slots.append((lambda c: jnp.where(c == final, 0, -1), [a for _, a in held]))

    half = max(1, len(own) // 2)
    early = [(origin, arrays[:half]) for origin, arrays in slots]
    late = [(origin, arrays[half:]) for origin, arrays in slots]
    q_parts[0], gate_row = lax.optimization_barrier((q_parts[0], gate_row))
    states = []
    for d in range(splits):
        states.append(attend(q_parts[d], early, span_mask, None, False))

    columns = out_weight.shape[1]
    width = columns // COL_BLOCKS
    project = lambda a, w: jnp.dot(a, w, preferred_element_type=jnp.float32).astype(jnp.bfloat16)
    returned = [[] for _ in range(COL_BLOCKS)]
    for d in range(1, splits):
        attended = attend(q_parts[d], late, span_mask, states[d], True)
        back = [((i + d) % splits, i) for i in range(splits)]
        for j in range(COL_BLOCKS):
            partial = project(attended, out_weight[:, j * width : (j + 1) * width])
            returned[j].append(permute(partial, "head", back))
    attended = attend(q_parts[0], late, span_mask, states[0], True)
    kept = lax.optimization_barrier(project(attended, out_weight))
    updated = hidden
    for j in range(COL_BLOCKS):
        cols = slice(j * width, (j + 1) * width)
        total = kept[:, cols].astype(jnp.float32)
        for a in returned[j]:
            total = total + a.astype(jnp.float32)
        fresh = updated[:, cols].astype(jnp.float32) + gate_row[None, cols] * total
        updated = lax.dynamic_update_slice_in_dim(updated, fresh.astype(jnp.bfloat16), j * width, 1)
    return updated


def solution(mesh):
    sizes = (mesh.shape["tm"], mesh.shape["head"], mesh.shape["branch"])
    return jax.shard_map(
        functools.partial(body, sizes),
        mesh=mesh,
        in_specs=(
            P("branch", "tm", "head", None, None),
            P("branch", "tm", "head", None, None),
            P("branch", "tm", "head", None, None),
            P("tm", ("head", "branch"), None, None),
            P("tm", ("head", "branch"), None, None),
            P("branch", "tm", "head", None),
            P("head", None),
            P(),
            P(),
            P(),
            P(),
        ),
        out_specs=P("branch", "tm", "head", None),
        check_vma=False,
    )
```

```python
import functools
import math

import jax
import jax.numpy as jnp
from jax import lax
from jax.experimental import pallas as pl
from jax.experimental.pallas import tpu as pltpu
from jax.sharding import PartitionSpec as P

NEG_BIG = -1e30
LOG2E = 1.4426950408889634
COL_BLOCKS = 5
HEAD_STEP_SCORES = 2 << 20
VMEM_LIMIT = 28 << 20


def hidden_bias(mask, span, origin):
    source = origin(span)
    return jnp.where((source >= 0) & (mask[span, jnp.maximum(source, 0)] > 0), 0.0, NEG_BIG)


def flash_kernel(mask, *refs, layout, count, scale, step, first, last):
    q_ref, kv_refs, refs = refs[0], refs[1 : 1 + count], refs[1 + count :]
    span = lax.axis_index("tm")
    odd = lax.rem(span, 2) == 1
    biases = [None if origin is None else hidden_bias(mask, span, origin) for origin, _ in layout]

    def gather(kind, h):
        blocks = []
        for _, members in layout:
            for choices, _ in members:
                block = kv_refs[choices[0]][kind, h]
                if len(choices) > 1:
                    block = jnp.where(odd, block, kv_refs[choices[1]][kind, h])
                blocks.append(block)
        return jnp.concatenate(blocks, axis=0)

    if not first:
        (max_in, sum_in, acc_in), refs = refs[:3], refs[3:]
    outs, score_ref = refs[:-1], refs[-1]
    dim = q_ref.shape[2]
    order = [(bias, size) for bias, (_, members) in zip(biases, layout) for _, size in members]
    for h in range(step):
        raw = lax.dot_general(
            q_ref[h], gather(0, h), (((1,), (1,)), ((), ())), preferred_element_type=jnp.float32
        )
        at, top = 0, None
        for bias, size in order:
            for _ in range(0, size, dim):
                piece = raw[:, at : at + dim]
                if bias is not None:
                    piece = piece + bias
                score_ref[h, :, at : at + dim] = piece
                top = piece if top is None else jnp.maximum(top, piece)
                at += dim
        top = jnp.broadcast_to(jnp.max(top, axis=1, keepdims=True) * scale, top.shape)
        total = acc = None
        if not first:
            old = max_in[h]
            top = jnp.maximum(top, old)
            shrink = jnp.exp2(old - top)
            total, acc = sum_in[h] * shrink, acc_in[h] * shrink
        weights = []
        for j in range(0, at, dim):
            piece = jnp.exp2(score_ref[h, :, j : j + dim] * scale - top)
            total = piece if total is None else total + piece
            weights.append(piece.astype(jnp.bfloat16))
        added = jnp.dot(
            jnp.concatenate(weights, axis=1), gather(1, h), preferred_element_type=jnp.float32
        )
        acc = added if acc is None else acc + added
        if last:
            total = jnp.sum(total, axis=1, keepdims=True)
            outs[0][:, h * dim : (h + 1) * dim] = (acc / total).astype(outs[0].dtype)
        else:
            outs[0][h], outs[1][h], outs[2][h] = top, total, acc


def attend(queries, slots, span_mask, state, last):
    heads, rows, dim = queries.shape
    arrays, layout = [], []
    for origin, members in slots:
        places = []
        for member in members:
            choices = member if isinstance(member, tuple) else (member,)
            places.append((tuple(range(len(arrays), len(arrays) + len(choices))), choices[0].shape[2]))
            arrays += choices
        layout.append((origin, places))
    keys = sum(size for _, places in layout for _, size in places)
    step = max(s for s in range(1, heads + 1) if heads % s == 0 and s * rows * keys <= HEAD_STEP_SCORES)
    by_head = pl.BlockSpec((step, rows, dim), lambda h, f: (h, 0, 0))
    states = [] if state is None else list(state)
    return pl.pallas_call(
        functools.partial(
            flash_kernel,
            layout=layout,
            count=len(arrays),
            scale=LOG2E / math.sqrt(dim),
            step=step,
            first=state is None,
            last=last,
        ),
        out_shape=jax.ShapeDtypeStruct((rows, heads * dim), jnp.bfloat16)
        if last
        else [jax.ShapeDtypeStruct((heads, rows, dim), jnp.float32)] * 3,
        grid_spec=pltpu.PrefetchScalarGridSpec(
            num_scalar_prefetch=1,
            grid=(heads // step,),
            in_specs=[by_head]
            + [
                pl.BlockSpec((2, step, array.shape[2], dim), lambda h, f: (0, h, 0, 0))
                for array in arrays
            ]
            + [by_head] * len(states),
            out_specs=pl.BlockSpec((rows, step * dim), lambda h, f: (0, h)) if last else [by_head] * 3,
            scratch_shapes=[pltpu.VMEM((step, rows, keys), jnp.float32)],
        ),
        cost_estimate=pl.CostEstimate(
            flops=4 * heads * rows * keys * dim,
            bytes_accessed=2 * heads * dim * (2 * rows + 2 * keys),
            transcendentals=heads * rows * keys,
        ),
        compiler_params=pltpu.CompilerParams(vmem_limit_bytes=VMEM_LIMIT),
    )(span_mask, queries, *arrays, *states)


def body(sizes, queries, keys, values, ctx_keys, ctx_values, hidden, out_weight, gates, levels, span_mask, prefix):
    return sublayer(
        sizes, queries[0, 0], keys[0, 0], values[0, 0], ctx_keys[0], ctx_values[0], hidden[0, 0],
        out_weight, gates, levels, span_mask, prefix,
    )[None, None]


def sublayer(sizes, queries, keys, values, ctx_keys, ctx_values, hidden, out_weight, gates, levels, span_mask, prefix):
    spans, splits, branches = sizes
    span = lax.axis_index("tm")
    part = lax.axis_index("head")
    to_heads = lambda a: jnp.transpose(a, (1, 0, 2))
    q, k, v = to_heads(queries), to_heads(keys), to_heads(values)
    ck, cv = to_heads(ctx_keys), to_heads(ctx_values)
    group = q.shape[0] // splits
    take = lambda a, d: lax.dynamic_slice_in_dim(a, lax.rem(part + d, splits) * group, group, 0)
    pair = lambda a, b, d: jnp.stack([take(a, d), take(b, d)])
    cycle = lambda d: [(i, (i + d) % splits) for i in range(splits)]

    level_now = lax.dynamic_index_in_dim(levels, span, 0, keepdims=False)
    gate_row = lax.dynamic_index_in_dim(gates, level_now, 0, keepdims=False)

    ctx_parts, kv_parts, q_parts = [pair(ck, cv, 0)], [pair(k, v, 0)], [take(q, 0)]
    for d in range(1, splits):
        ctx_parts.append(lax.ppermute(pair(ck, cv, d), "head", cycle(d)))
    for d in range(1, splits):
        kv_parts.append(lax.ppermute(pair(k, v, d), "head", cycle(d)))
    for d in range(1, splits):
        q_parts.append(lax.ppermute(take(q, d), "head", cycle(d)))

    use_context = span < prefix[0]
    final = spans - 1
    stands_in = span == final
    lent = [lax.ppermute(a, "tm", [(0, final)]) for a in ctx_parts]
    pieces = [jnp.concatenate([jnp.where(stands_in, b, a) for a, b in zip(ctx_parts, lent)], axis=2)]
    piece_rows = pieces[0].shape[2]
    for i in range(1, branches):
        low = i & -i
        pieces.append(lax.ppermute(pieces[i - low], "branch", [(b, b ^ low) for b in range(branches)]))
    groups = [[i for i in range(branches) if i.bit_count() == n] for n in range(branches.bit_length())]
    rows, at, own, passed, held = k.shape[1], 0, [], [], []
    for members in groups:
        contexts = [pieces[i] for i in members]
        if own:
            held[-1], *contexts = lax.optimization_barrier(((own[-1], passed[-1]), *contexts))
        mine = []
        for _ in members:
            d, row = divmod(at, rows)
            mine.append(kv_parts[d][:, :, row : row + piece_rows])
            at += piece_rows
        context, mine = jnp.concatenate(contexts, axis=2), jnp.concatenate(mine, axis=2)
        own.append(jnp.where(use_context, context, mine))
        passed.append(jnp.where(use_context | stands_in, context, mine))
        held.append((own[-1], passed[-1]))

    pairs = [(i, i + 1) for i in range(0, spans, 2)]
    beside = [lax.ppermute(a, "tm", pairs + [(final, final - 1)]) for a in passed]
    slots = [
        (None, [a for a, _ in held]),
        (lambda c: jnp.where(lax.rem(c, 2) == 1, c - 1, jnp.where(c == final - 1, 0, -1)), beside),
    ]
    for s in range(2, final - 1, 2):
        far = [lax.ppermute(a, "tm", [(i, i + s) for i in range(spans - s)]) for a in own]
        back = [(b, a) for a, b in pairs]
        near = [lax.ppermute(a, "tm", pairs + back) for a in far]
        slots.append((lambda c, s=s: c - s, far))
        slots.append((lambda c, s=s: c + 1 - 2 * lax.rem(c, 2) - s, near))
    s = final - 1
    far = [lax.ppermute(a, "tm", [(1, final)]) for a in own]
    near = [lax.ppermute(a, "tm", [(final, final - 1)]) for a in far]
    slots.append((lambda c: jnp.where(c >= final - 1, 1, -1), list(zip(far, near))))
    slots.append((lambda c: jnp.where(c == final, 0, -1), [a for _, a in held]))

    early = [(origin, arrays[:-1]) for origin, arrays in slots]
    late = [(origin, arrays[-1:]) for origin, arrays in slots]
    q_parts[0], gate_row = lax.optimization_barrier((q_parts[0], gate_row))
    states = {}
    for d in range(1, splits):
        states[d] = attend(q_parts[d], early, span_mask, None, False)

    columns = out_weight.shape[1]
    width = columns // COL_BLOCKS
    project = lambda a, w: jnp.dot(a, w, preferred_element_type=jnp.float32).astype(jnp.bfloat16)
    returned = [[] for _ in range(COL_BLOCKS)]
    for d in range(1, splits):
        attended = attend(q_parts[d], late, span_mask, states[d], True)
        back = [((i + d) % splits, i) for i in range(splits)]
        for j in range(COL_BLOCKS):
            partial = project(attended, out_weight[:, j * width : (j + 1) * width])
            returned[j].append(lax.ppermute(partial, "head", back))
    attended = attend(q_parts[0], slots, span_mask, None, True)
    kept = lax.optimization_barrier(project(attended, out_weight))
    updated = hidden
    for j in range(COL_BLOCKS):
        cols = slice(j * width, (j + 1) * width)
        total = kept[:, cols].astype(jnp.float32)
        for a in returned[j]:
            total = total + a.astype(jnp.float32)
        fresh = updated[:, cols].astype(jnp.float32) + gate_row[None, cols] * total
        updated = lax.dynamic_update_slice_in_dim(updated, fresh.astype(jnp.bfloat16), j * width, 1)
    return updated


def solution(mesh):
    sizes = (mesh.shape["tm"], mesh.shape["head"], mesh.shape["branch"])
    return jax.shard_map(
        functools.partial(body, sizes),
        mesh=mesh,
        in_specs=(
            P("branch", "tm", "head", None, None),
            P("branch", "tm", "head", None, None),
            P("branch", "tm", "head", None, None),
            P("tm", ("head", "branch"), None, None),
            P("tm", ("head", "branch"), None, None),
            P("branch", "tm", "head", None),
            P("head", None),
            P(),
            P(),
            P(),
            P(),
        ),
        out_specs=P("branch", "tm", "head", None),
        check_vma=False,
    )
```

```python
import functools
import math

import jax
import jax.numpy as jnp
from jax import lax
from jax.experimental import pallas as pl
from jax.experimental.pallas import tpu as pltpu
from jax.sharding import PartitionSpec as P

NEG_BIG = -1e30
LOG2E = 1.4426950408889634
COL_BLOCKS = 5
HEAD_STEP_SCORES = 2 << 20
VMEM_LIMIT = 28 << 20


def hidden_bias(mask, span, origin):
    source = origin(span)
    return jnp.where((source >= 0) & (mask[span, jnp.maximum(source, 0)] > 0), 0.0, NEG_BIG)


def flash_kernel(mask, *refs, layout, count, scale, step, first, last):
    q_ref, kv_refs, refs = refs[0], refs[1 : 1 + count], refs[1 + count :]
    span = lax.axis_index("tm")
    odd = lax.rem(span, 2) == 1
    biases = [None if origin is None else hidden_bias(mask, span, origin) for origin, _ in layout]

    def gather(kind, h):
        blocks = []
        for _, members in layout:
            for choices, _ in members:
                block = kv_refs[choices[0]][kind, h]
                if len(choices) > 1:
                    block = jnp.where(odd, block, kv_refs[choices[1]][kind, h])
                blocks.append(block)
        return jnp.concatenate(blocks, axis=0)

    if not first:
        (max_in, sum_in, acc_in), refs = refs[:3], refs[3:]
    outs, score_ref = refs[:-1], refs[-1]
    dim = q_ref.shape[2]
    order = [(bias, size) for bias, (_, members) in zip(biases, layout) for _, size in members]
    for h in range(step):
        raw = lax.dot_general(
            q_ref[h], gather(0, h), (((1,), (1,)), ((), ())), preferred_element_type=jnp.float32
        )
        at, top = 0, None
        for bias, size in order:
            for _ in range(0, size, dim):
                piece = raw[:, at : at + dim]
                if bias is not None:
                    piece = piece + bias
                score_ref[h, :, at : at + dim] = piece
                top = piece if top is None else jnp.maximum(top, piece)
                at += dim
        top = jnp.broadcast_to(jnp.max(top, axis=1, keepdims=True) * scale, top.shape)
        total = acc = None
        if not first:
            old = max_in[h]
            top = jnp.maximum(top, old)
            shrink = jnp.exp2(old - top)
            total, acc = sum_in[h] * shrink, acc_in[h] * shrink
        weights = []
        for j in range(0, at, dim):
            piece = jnp.exp2(score_ref[h, :, j : j + dim] * scale - top)
            total = piece if total is None else total + piece
            weights.append(piece.astype(jnp.bfloat16))
        added = jnp.dot(
            jnp.concatenate(weights, axis=1), gather(1, h), preferred_element_type=jnp.float32
        )
        acc = added if acc is None else acc + added
        if last:
            total = jnp.sum(total, axis=1, keepdims=True)
            outs[0][:, h * dim : (h + 1) * dim] = (acc / total).astype(outs[0].dtype)
        else:
            outs[0][h], outs[1][h], outs[2][h] = top, total, acc


def attend(queries, slots, span_mask, state, last):
    heads, rows, dim = queries.shape
    arrays, layout = [], []
    for origin, members in slots:
        places = []
        for member in members:
            choices = member if isinstance(member, tuple) else (member,)
            places.append((tuple(range(len(arrays), len(arrays) + len(choices))), choices[0].shape[2]))
            arrays += choices
        layout.append((origin, places))
    keys = sum(size for _, places in layout for _, size in places)
    step = max(s for s in range(1, heads + 1) if heads % s == 0 and s * rows * keys <= HEAD_STEP_SCORES)
    by_head = pl.BlockSpec((step, rows, dim), lambda h, f: (h, 0, 0))
    states = [] if state is None else list(state)
    return pl.pallas_call(
        functools.partial(
            flash_kernel,
            layout=layout,
            count=len(arrays),
            scale=LOG2E / math.sqrt(dim),
            step=step,
            first=state is None,
            last=last,
        ),
        out_shape=jax.ShapeDtypeStruct((rows, heads * dim), jnp.bfloat16)
        if last
        else [jax.ShapeDtypeStruct((heads, rows, dim), jnp.float32)] * 3,
        grid_spec=pltpu.PrefetchScalarGridSpec(
            num_scalar_prefetch=1,
            grid=(heads // step,),
            in_specs=[by_head]
            + [
                pl.BlockSpec((2, step, array.shape[2], dim), lambda h, f: (0, h, 0, 0))
                for array in arrays
            ]
            + [by_head] * len(states),
            out_specs=pl.BlockSpec((rows, step * dim), lambda h, f: (0, h)) if last else [by_head] * 3,
            scratch_shapes=[pltpu.VMEM((step, rows, keys), jnp.float32)],
        ),
        cost_estimate=pl.CostEstimate(
            flops=4 * heads * rows * keys * dim,
            bytes_accessed=2 * heads * dim * (2 * rows + 2 * keys),
            transcendentals=heads * rows * keys,
        ),
        compiler_params=pltpu.CompilerParams(vmem_limit_bytes=VMEM_LIMIT),
    )(span_mask, queries, *arrays, *states)


def body(sizes, queries, keys, values, ctx_keys, ctx_values, hidden, out_weight, gates, levels, span_mask, prefix):
    return sublayer(
        sizes, queries[0, 0], keys[0, 0], values[0, 0], ctx_keys[0], ctx_values[0], hidden[0, 0],
        out_weight, gates, levels, span_mask, prefix,
    )[None, None]


def sublayer(sizes, queries, keys, values, ctx_keys, ctx_values, hidden, out_weight, gates, levels, span_mask, prefix):
    spans, splits, branches = sizes
    span = lax.axis_index("tm")
    part = lax.axis_index("head")
    to_heads = lambda a: jnp.transpose(a, (1, 0, 2))
    q, k, v = to_heads(queries), to_heads(keys), to_heads(values)
    ck, cv = to_heads(ctx_keys), to_heads(ctx_values)
    group = q.shape[0] // splits
    take = lambda a, d: lax.dynamic_slice_in_dim(a, lax.rem(part + d, splits) * group, group, 0)
    pair = lambda a, b, d: jnp.stack([take(a, d), take(b, d)])
    cycle = lambda d: [(i, (i + d) % splits) for i in range(splits)]


    ctx_parts, kv_parts, q_parts = [pair(ck, cv, 0)], [pair(k, v, 0)], [take(q, 0)]
    for d in range(1, splits):
        ctx_parts.append(lax.ppermute(pair(ck, cv, d), "head", cycle(d)))
    for d in range(1, splits):
        kv_parts.append(lax.ppermute(pair(k, v, d), "head", cycle(d)))
    for d in range(1, splits):
        q_parts.append(lax.ppermute(take(q, d), "head", cycle(d)))

    use_context = span < prefix[0]
    final = spans - 1
    stands_in = span == final
    lent = [lax.ppermute(a, "tm", [(0, final)]) for a in ctx_parts]
    pieces = [jnp.concatenate([jnp.where(stands_in, b, a) for a, b in zip(ctx_parts, lent)], axis=2)]
    piece_rows = pieces[0].shape[2]
    for i in range(1, branches):
        low = i & -i
        pieces.append(lax.ppermute(pieces[i - low], "branch", [(b, b ^ low) for b in range(branches)]))
    groups = [[i for i in range(branches) if i.bit_count() == n] for n in range(branches.bit_length())]
    rows, at, own, passed, held = k.shape[1], 0, [], [], []
    for members in groups:
        contexts = [pieces[i] for i in members]
        if own:
            held[-1], *contexts = lax.optimization_barrier(((own[-1], passed[-1]), *contexts))
        mine = []
        for _ in members:
            d, row = divmod(at, rows)
            mine.append(kv_parts[d][:, :, row : row + piece_rows])
            at += piece_rows
        context, mine = jnp.concatenate(contexts, axis=2), jnp.concatenate(mine, axis=2)
        own.append(jnp.where(use_context, context, mine))
        passed.append(jnp.where(use_context | stands_in, context, mine))
        held.append((own[-1], passed[-1]))

    pairs = [(i, i + 1) for i in range(0, spans, 2)]
    beside = [lax.ppermute(a, "tm", pairs + [(final, final - 1)]) for a in passed]
    slots = [
        (None, [a for a, _ in held]),
        (lambda c: jnp.where(lax.rem(c, 2) == 1, c - 1, jnp.where(c == final - 1, 0, -1)), beside),
    ]
    for s in range(2, final - 1, 2):
        far = [lax.ppermute(a, "tm", [(i, i + s) for i in range(spans - s)]) for a in own]
        back = [(b, a) for a, b in pairs]
        near = [lax.ppermute(a, "tm", pairs + back) for a in far]
        slots.append((lambda c, s=s: c - s, far))
        slots.append((lambda c, s=s: c + 1 - 2 * lax.rem(c, 2) - s, near))
    s = final - 1
    far = [lax.ppermute(a, "tm", [(1, final)]) for a in own]
    near = [lax.ppermute(a, "tm", [(final, final - 1)]) for a in far]
    slots.append((lambda c: jnp.where(c >= final - 1, 1, -1), list(zip(far, near))))
    slots.append((lambda c: jnp.where(c == final, 0, -1), [a for _, a in held]))

    cuts = [len(groups) - 1 if i in (0, 1, len(slots) - 1) else len(groups) - 2 for i in range(len(slots))]
    early = [(origin, arrays[:cut]) for (origin, arrays), cut in zip(slots, cuts)]
    late = [(origin, arrays[cut:]) for (origin, arrays), cut in zip(slots, cuts)]
    states = {}
    for d in range(1, splits):
        states[d] = attend(q_parts[d], early, span_mask, None, False)

    columns = out_weight.shape[1]
    width = columns // COL_BLOCKS
    project = lambda a, w: jnp.dot(a, w, preferred_element_type=jnp.float32).astype(jnp.bfloat16)
    returned = [[] for _ in range(COL_BLOCKS)]
    for d in range(1, splits):
        attended = attend(q_parts[d], late, span_mask, states[d], True)
        back = [((i + d) % splits, i) for i in range(splits)]
        for j in range(COL_BLOCKS):
            partial = project(attended, out_weight[:, j * width : (j + 1) * width])
            returned[j].append(lax.ppermute(partial, "head", back))
    attended = attend(q_parts[0], slots, span_mask, None, True)
    attended, levels = lax.optimization_barrier((attended, levels))
    level_now = lax.dynamic_index_in_dim(levels, span, 0, keepdims=False)
    gate_row = lax.dynamic_index_in_dim(gates, level_now, 0, keepdims=False)
    kept = lax.optimization_barrier(project(attended, out_weight))
    updated = hidden
    for j in range(COL_BLOCKS):
        cols = slice(j * width, (j + 1) * width)
        total = kept[:, cols].astype(jnp.float32)
        for a in returned[j]:
            total = total + a.astype(jnp.float32)
        fresh = updated[:, cols].astype(jnp.float32) + gate_row[None, cols] * total
        updated = lax.dynamic_update_slice_in_dim(updated, fresh.astype(jnp.bfloat16), j * width, 1)
    return updated


def solution(mesh):
    sizes = (mesh.shape["tm"], mesh.shape["head"], mesh.shape["branch"])
    return jax.shard_map(
        functools.partial(body, sizes),
        mesh=mesh,
        in_specs=(
            P("branch", "tm", "head", None, None),
            P("branch", "tm", "head", None, None),
            P("branch", "tm", "head", None, None),
            P("tm", ("head", "branch"), None, None),
            P("tm", ("head", "branch"), None, None),
            P("branch", "tm", "head", None),
            P("head", None),
            P(),
            P(),
            P(),
            P(),
        ),
        out_specs=P("branch", "tm", "head", None),
        check_vma=False,
    )
```

```python
import functools
import math

import jax
import jax.numpy as jnp
from jax import lax
from jax.experimental import pallas as pl
from jax.experimental.pallas import tpu as pltpu
from jax.sharding import PartitionSpec as P

NEG_BIG = -1e30
LOG2E = 1.4426950408889634
COL_BLOCKS = 5
HEAD_STEP_SCORES = 1 << 20
VMEM_MARGIN = 3 << 20


def hidden_bias(mask, span, origin):
    source = origin(span)
    return jnp.where((source >= 0) & (mask[span, jnp.maximum(source, 0)] > 0), 0.0, NEG_BIG)


def flash_kernel(mask, *refs, layout, count, scale, step, first, last):
    q_ref, kv_refs, refs = refs[0], refs[1 : 1 + count], refs[1 + count :]
    span = lax.axis_index("tm")
    odd = lax.rem(span, 2) == 1
    biases = [None if origin is None else hidden_bias(mask, span, origin) for origin, _ in layout]

    def gather(kind, h):
        blocks = []
        for _, members in layout:
            for choices, _ in members:
                block = kv_refs[choices[0]][kind, h]
                if len(choices) > 1:
                    block = jnp.where(odd, block, kv_refs[choices[1]][kind, h])
                blocks.append(block)
        return jnp.concatenate(blocks, axis=0)

    if not first:
        (max_in, sum_in, acc_in), refs = refs[:3], refs[3:]
    outs, score_ref = refs[:-1], refs[-1]
    dim = q_ref.shape[2]
    order = [(bias, size) for bias, (_, members) in zip(biases, layout) for _, size in members]
    for h in range(step):
        raw = lax.dot_general(
            q_ref[h], gather(0, h), (((1,), (1,)), ((), ())), preferred_element_type=jnp.float32
        )
        at, top = 0, None
        for bias, size in order:
            for _ in range(0, size, dim):
                piece = raw[:, at : at + dim]
                if bias is not None:
                    piece = piece + bias
                score_ref[h, :, at : at + dim] = piece
                top = piece if top is None else jnp.maximum(top, piece)
                at += dim
        top = jnp.broadcast_to(jnp.max(top, axis=1, keepdims=True) * scale, top.shape)
        total = acc = None
        if not first:
            old = max_in[h]
            top = jnp.maximum(top, old)
            shrink = jnp.exp2(old - top)
            total, acc = sum_in[h] * shrink, acc_in[h] * shrink
        weights = []
        for j in range(0, at, dim):
            piece = jnp.exp2(score_ref[h, :, j : j + dim] * scale - top)
            total = piece if total is None else total + piece
            weights.append(piece.astype(jnp.bfloat16))
        added = jnp.dot(
            jnp.concatenate(weights, axis=1), gather(1, h), preferred_element_type=jnp.float32
        )
        acc = added if acc is None else acc + added
        if last:
            total = jnp.sum(total, axis=1, keepdims=True)
            outs[0][:, h * dim : (h + 1) * dim] = (acc / total).astype(outs[0].dtype)
        else:
            outs[0][h], outs[1][h], outs[2][h] = top, total, acc


def attend(queries, slots, span_mask, state, last):
    heads, rows, dim = queries.shape
    arrays, layout = [], []
    for origin, members in slots:
        places = []
        for member in members:
            choices = member if isinstance(member, tuple) else (member,)
            places.append((tuple(range(len(arrays), len(arrays) + len(choices))), choices[0].shape[2]))
            arrays += choices
        layout.append((origin, places))
    keys = sum(size for _, places in layout for _, size in places)
    step = max(s for s in range(1, heads + 1) if heads % s == 0 and s * rows * keys <= HEAD_STEP_SCORES)
    read = sum(array.shape[2] for array in arrays)
    blocks = step * dim * (2 * 2 * read + 2 * 2 * rows + 3 * 4 * rows)
    grant = 4 * step * rows * keys + 2 * blocks + VMEM_MARGIN
    by_head = pl.BlockSpec((step, rows, dim), lambda h, f: (h, 0, 0))
    states = [] if state is None else list(state)
    return pl.pallas_call(
        functools.partial(
            flash_kernel,
            layout=layout,
            count=len(arrays),
            scale=LOG2E / math.sqrt(dim),
            step=step,
            first=state is None,
            last=last,
        ),
        out_shape=jax.ShapeDtypeStruct((rows, heads * dim), jnp.bfloat16)
        if last
        else [jax.ShapeDtypeStruct((heads, rows, dim), jnp.float32)] * 3,
        grid_spec=pltpu.PrefetchScalarGridSpec(
            num_scalar_prefetch=1,
            grid=(heads // step,),
            in_specs=[by_head]
            + [
                pl.BlockSpec((2, step, array.shape[2], dim), lambda h, f: (0, h, 0, 0))
                for array in arrays
            ]
            + [by_head] * len(states),
            out_specs=pl.BlockSpec((rows, step * dim), lambda h, f: (0, h)) if last else [by_head] * 3,
            scratch_shapes=[pltpu.VMEM((step, rows, keys), jnp.float32)],
        ),
        cost_estimate=pl.CostEstimate(
            flops=4 * heads * rows * keys * dim,
            bytes_accessed=2 * heads * dim * (2 * rows + 2 * keys),
            transcendentals=heads * rows * keys,
        ),
        compiler_params=pltpu.CompilerParams(vmem_limit_bytes=grant),
    )(span_mask, queries, *arrays, *states)


def body(sizes, queries, keys, values, ctx_keys, ctx_values, hidden, out_weight, gates, levels, span_mask, prefix):
    return sublayer(
        sizes, queries[0, 0], keys[0, 0], values[0, 0], ctx_keys[0], ctx_values[0], hidden[0, 0],
        out_weight, gates, levels, span_mask, prefix,
    )[None, None]


def sublayer(sizes, queries, keys, values, ctx_keys, ctx_values, hidden, out_weight, gates, levels, span_mask, prefix):
    spans, splits, branches = sizes
    span = lax.axis_index("tm")
    part = lax.axis_index("head")
    to_heads = lambda a: jnp.transpose(a, (1, 0, 2))
    q, k, v = to_heads(queries), to_heads(keys), to_heads(values)
    ck, cv = to_heads(ctx_keys), to_heads(ctx_values)
    group = q.shape[0] // splits
    take = lambda a, d: lax.dynamic_slice_in_dim(a, lax.rem(part + d, splits) * group, group, 0)
    pair = lambda a, b, d: jnp.stack([take(a, d), take(b, d)])
    cycle = lambda d: [(i, (i + d) % splits) for i in range(splits)]


    ctx_parts, kv_parts, q_parts = [pair(ck, cv, 0)], [pair(k, v, 0)], [take(q, 0)]
    for d in range(1, splits):
        ctx_parts.append(lax.ppermute(pair(ck, cv, d), "head", cycle(d)))
    for d in range(1, splits):
        kv_parts.append(lax.ppermute(pair(k, v, d), "head", cycle(d)))
    for d in range(1, splits):
        q_parts.append(lax.ppermute(take(q, d), "head", cycle(d)))

    use_context = span < prefix[0]
    level_now = lax.dynamic_index_in_dim(levels, span, 0, keepdims=False)
    gate_row = lax.dynamic_index_in_dim(gates, level_now, 0, keepdims=False)
    final = spans - 1
    stands_in = span == final
    ctx_parts[0], gate_row = lax.optimization_barrier((ctx_parts[0], gate_row))
    lent = [lax.ppermute(a, "tm", [(0, final)]) for a in ctx_parts]
    pieces = [jnp.concatenate([jnp.where(stands_in, b, a) for a, b in zip(ctx_parts, lent)], axis=2)]
    piece_rows = pieces[0].shape[2]
    for i in range(1, branches):
        low = i & -i
        pieces.append(lax.ppermute(pieces[i - low], "branch", [(b, b ^ low) for b in range(branches)]))
    groups = [[i for i in range(branches) if i.bit_count() == n] for n in range(branches.bit_length())]
    rows, at, own, passed, held = k.shape[1], 0, [], [], []
    for members in groups:
        contexts = [pieces[i] for i in members]
        if own:
            held[-1], *contexts = lax.optimization_barrier(((own[-1], passed[-1]), *contexts))
        mine = []
        for _ in members:
            d, row = divmod(at, rows)
            mine.append(kv_parts[d][:, :, row : row + piece_rows])
            at += piece_rows
        context, mine = jnp.concatenate(contexts, axis=2), jnp.concatenate(mine, axis=2)
        own.append(jnp.where(use_context, context, mine))
        passed.append(jnp.where(use_context | stands_in, context, mine))
        held.append((own[-1], passed[-1]))

    pairs = [(i, i + 1) for i in range(0, spans, 2)]
    beside = [lax.ppermute(a, "tm", pairs + [(final, final - 1)]) for a in passed]
    slots = [
        (None, [a for a, _ in held]),
        (lambda c: jnp.where(lax.rem(c, 2) == 1, c - 1, jnp.where(c == final - 1, 0, -1)), beside),
    ]
    for s in range(2, final - 1, 2):
        far = [lax.ppermute(a, "tm", [(i, i + s) for i in range(spans - s)]) for a in own]
        back = [(b, a) for a, b in pairs]
        near = [lax.ppermute(a, "tm", pairs + back) for a in far]
        slots.append((lambda c, s=s: c - s, far))
        slots.append((lambda c, s=s: c + 1 - 2 * lax.rem(c, 2) - s, near))
    s = final - 1
    far = [lax.ppermute(a, "tm", [(1, final)]) for a in own]
    near = [lax.ppermute(a, "tm", [(final, final - 1)]) for a in far]
    slots.append((lambda c: jnp.where(c >= final - 1, 1, -1), list(zip(far, near))))
    slots.append((lambda c: jnp.where(c == final, 0, -1), [a for _, a in held]))

    cuts = [len(groups) - 1 if i in (0, 1, len(slots) - 1) else len(groups) - 2 for i in range(len(slots))]
    early = [(origin, arrays[:cut]) for (origin, arrays), cut in zip(slots, cuts)]
    late = [(origin, arrays[cut:]) for (origin, arrays), cut in zip(slots, cuts)]
    states = {}
    for d in range(1, splits):
        states[d] = attend(q_parts[d], early, span_mask, None, False)

    columns = out_weight.shape[1]
    width = columns // COL_BLOCKS
    project = lambda a, w: jnp.dot(a, w, preferred_element_type=jnp.float32).astype(jnp.bfloat16)
    returned = [[] for _ in range(COL_BLOCKS)]
    for d in range(1, splits):
        attended = attend(q_parts[d], late, span_mask, states[d], True)
        back = [((i + d) % splits, i) for i in range(splits)]
        for j in range(COL_BLOCKS):
            partial = project(attended, out_weight[:, j * width : (j + 1) * width])
            returned[j].append(lax.ppermute(partial, "head", back))
    attended = attend(q_parts[0], slots, span_mask, None, True)
    kept = lax.optimization_barrier(project(attended, out_weight))
    updated = hidden
    for j in range(COL_BLOCKS):
        cols = slice(j * width, (j + 1) * width)
        total = kept[:, cols].astype(jnp.float32)
        for a in returned[j]:
            total = total + a.astype(jnp.float32)
        fresh = updated[:, cols].astype(jnp.float32) + gate_row[None, cols] * total
        updated = lax.dynamic_update_slice_in_dim(updated, fresh.astype(jnp.bfloat16), j * width, 1)
    return updated


def solution(mesh):
    sizes = (mesh.shape["tm"], mesh.shape["head"], mesh.shape["branch"])
    return jax.shard_map(
        functools.partial(body, sizes),
        mesh=mesh,
        in_specs=(
            P("branch", "tm", "head", None, None),
            P("branch", "tm", "head", None, None),
            P("branch", "tm", "head", None, None),
            P("tm", ("head", "branch"), None, None),
            P("tm", ("head", "branch"), None, None),
            P("branch", "tm", "head", None),
            P("head", None),
            P(),
            P(),
            P(),
            P(),
        ),
        out_specs=P("branch", "tm", "head", None),
        check_vma=False,
    )
```

```python
import functools
import math

import jax
import jax.numpy as jnp
from jax import lax
from jax.experimental import pallas as pl
from jax.experimental.pallas import tpu as pltpu
from jax.sharding import PartitionSpec as P

NEG_BIG = -1e30
LOG2E = 1.4426950408889634
COL_BLOCKS = 5
HEAD_STEP_SCORES = 1 << 20
VMEM_MARGIN = 3 << 20


def hidden_bias(mask, span, origin):
    source = origin(span)
    return jnp.where((source >= 0) & (mask[span, jnp.maximum(source, 0)] > 0), 0.0, NEG_BIG)


def flash_kernel(mask, *refs, layout, count, scale, step, first, last):
    q_ref, kv_refs, refs = refs[0], refs[1 : 1 + count], refs[1 + count :]
    span = lax.axis_index("tm")
    odd = lax.rem(span, 2) == 1
    biases = [None if origin is None else hidden_bias(mask, span, origin) for origin, _ in layout]

    def gather(kind, h):
        blocks = []
        for _, members in layout:
            for choices, _ in members:
                block = kv_refs[choices[0]][kind, h]
                if len(choices) > 1:
                    block = jnp.where(odd, block, kv_refs[choices[1]][kind, h])
                blocks.append(block)
        return jnp.concatenate(blocks, axis=0)

    if not first:
        (max_in, sum_in, acc_in), refs = refs[:3], refs[3:]
    outs, score_ref = refs[:-1], refs[-1]
    dim = q_ref.shape[2]
    order = [(bias, size) for bias, (_, members) in zip(biases, layout) for _, size in members]
    for h in range(step):
        raw = lax.dot_general(
            q_ref[h], gather(0, h), (((1,), (1,)), ((), ())), preferred_element_type=jnp.float32
        )
        at, top = 0, None
        for bias, size in order:
            for _ in range(0, size, dim):
                piece = raw[:, at : at + dim]
                if bias is not None:
                    piece = piece + bias
                score_ref[h, :, at : at + dim] = piece
                top = piece if top is None else jnp.maximum(top, piece)
                at += dim
        top = jnp.broadcast_to(jnp.max(top, axis=1, keepdims=True) * scale, top.shape)
        total = acc = None
        if not first:
            old = max_in[h]
            top = jnp.maximum(top, old)
            shrink = jnp.exp2(old - top)
            total, acc = sum_in[h] * shrink, acc_in[h] * shrink
        weights = []
        for j in range(0, at, dim):
            piece = jnp.exp2(score_ref[h, :, j : j + dim] * scale - top)
            total = piece if total is None else total + piece
            weights.append(piece.astype(jnp.bfloat16))
        added = jnp.dot(
            jnp.concatenate(weights, axis=1), gather(1, h), preferred_element_type=jnp.float32
        )
        acc = added if acc is None else acc + added
        if last:
            total = jnp.sum(total, axis=1, keepdims=True)
            outs[0][:, h * dim : (h + 1) * dim] = (acc / total).astype(outs[0].dtype)
        else:
            outs[0][h], outs[1][h], outs[2][h] = top, total, acc


def attend(queries, slots, span_mask, state, last):
    heads, rows, dim = queries.shape
    arrays, layout = [], []
    for origin, members in slots:
        places = []
        for member in members:
            choices = member if isinstance(member, tuple) else (member,)
            places.append((tuple(range(len(arrays), len(arrays) + len(choices))), choices[0].shape[2]))
            arrays += choices
        layout.append((origin, places))
    keys = sum(size for _, places in layout for _, size in places)
    step = max(s for s in range(1, heads + 1) if heads % s == 0 and s * rows * keys <= HEAD_STEP_SCORES)
    read = sum(array.shape[2] for array in arrays)
    blocks = step * dim * (2 * 2 * read + 2 * 2 * rows + 3 * 4 * rows)
    grant = 4 * step * rows * keys + 2 * blocks + VMEM_MARGIN
    by_head = pl.BlockSpec((step, rows, dim), lambda h, f: (h, 0, 0))
    states = [] if state is None else list(state)
    return pl.pallas_call(
        functools.partial(
            flash_kernel,
            layout=layout,
            count=len(arrays),
            scale=LOG2E / math.sqrt(dim),
            step=step,
            first=state is None,
            last=last,
        ),
        out_shape=jax.ShapeDtypeStruct((rows, heads * dim), jnp.bfloat16)
        if last
        else [jax.ShapeDtypeStruct((heads, rows, dim), jnp.float32)] * 3,
        grid_spec=pltpu.PrefetchScalarGridSpec(
            num_scalar_prefetch=1,
            grid=(heads // step,),
            in_specs=[by_head]
            + [
                pl.BlockSpec((2, step, array.shape[2], dim), lambda h, f: (0, h, 0, 0))
                for array in arrays
            ]
            + [by_head] * len(states),
            out_specs=pl.BlockSpec((rows, step * dim), lambda h, f: (0, h)) if last else [by_head] * 3,
            scratch_shapes=[pltpu.VMEM((step, rows, keys), jnp.float32)],
        ),
        cost_estimate=pl.CostEstimate(
            flops=4 * heads * rows * keys * dim,
            bytes_accessed=2 * heads * dim * (2 * rows + 2 * keys),
            transcendentals=heads * rows * keys,
        ),
        compiler_params=pltpu.CompilerParams(vmem_limit_bytes=grant),
    )(span_mask, queries, *arrays, *states)


def body(sizes, queries, keys, values, ctx_keys, ctx_values, hidden, out_weight, gates, levels, span_mask, prefix):
    return sublayer(
        sizes, queries[0, 0], keys[0, 0], values[0, 0], ctx_keys[0], ctx_values[0], hidden[0, 0],
        out_weight, gates, levels, span_mask, prefix,
    )[None, None]


def sublayer(sizes, queries, keys, values, ctx_keys, ctx_values, hidden, out_weight, gates, levels, span_mask, prefix):
    spans, splits, branches = sizes
    span = lax.axis_index("tm")
    part = lax.axis_index("head")
    to_heads = lambda a: jnp.transpose(a, (1, 0, 2))
    q, k, v = to_heads(queries), to_heads(keys), to_heads(values)
    ck, cv = to_heads(ctx_keys), to_heads(ctx_values)
    group = q.shape[0] // splits
    take = lambda a, d: lax.dynamic_slice_in_dim(a, lax.rem(part + d, splits) * group, group, 0)
    pair = lambda a, b, d: jnp.stack([take(a, d), take(b, d)])
    cycle = lambda d: [(i, (i + d) % splits) for i in range(splits)]


    ctx_parts, kv_parts, q_parts = [pair(ck, cv, 0)], [pair(k, v, 0)], [take(q, 0)]
    for d in range(1, splits):
        ctx_parts.append(lax.ppermute(pair(ck, cv, d), "head", cycle(d)))
    for d in range(1, splits):
        kv_parts.append(lax.ppermute(pair(k, v, d), "head", cycle(d)))
    for d in range(1, splits):
        q_parts.append(lax.ppermute(take(q, d), "head", cycle(d)))

    use_context = span < prefix[0]
    level_now = lax.dynamic_index_in_dim(levels, span, 0, keepdims=False)
    gate_row = lax.dynamic_index_in_dim(gates, level_now, 0, keepdims=False)
    final = spans - 1
    stands_in = span == final
    ctx_parts[0], gate_row = lax.optimization_barrier((ctx_parts[0], gate_row))
    lent = [lax.ppermute(a, "tm", [(0, final)]) for a in ctx_parts]
    pieces = [jnp.concatenate([jnp.where(stands_in, b, a) for a, b in zip(ctx_parts, lent)], axis=2)]
    piece_rows = pieces[0].shape[2]
    for i in range(1, branches):
        low = i & -i
        pieces.append(lax.ppermute(pieces[i - low], "branch", [(b, b ^ low) for b in range(branches)]))
    groups = [[i for i in range(branches) if i.bit_count() == n] for n in range(branches.bit_length())]
    rows, at, own, passed, held = k.shape[1], 0, [], [], []
    for members in groups:
        contexts = [pieces[i] for i in members]
        if own:
            held[-1], *contexts = lax.optimization_barrier(((own[-1], passed[-1]), *contexts))
        mine = []
        for _ in members:
            d, row = divmod(at, rows)
            mine.append(kv_parts[d][:, :, row : row + piece_rows])
            at += piece_rows
        context, mine = jnp.concatenate(contexts, axis=2), jnp.concatenate(mine, axis=2)
        own.append(jnp.where(use_context, context, mine))
        passed.append(jnp.where(use_context | stands_in, context, mine))
        held.append((own[-1], passed[-1]))

    pairs = [(i, i + 1) for i in range(0, spans, 2)]
    beside = [lax.ppermute(a, "tm", pairs + [(final, final - 1)]) for a in passed]
    slots = [
        (None, [a for a, _ in held]),
        (lambda c: jnp.where(lax.rem(c, 2) == 1, c - 1, jnp.where(c == final - 1, 0, -1)), beside),
    ]
    for s in range(2, final - 1, 2):
        far = [lax.ppermute(a, "tm", [(i, i + s) for i in range(spans - s)]) for a in own]
        back = [(b, a) for a, b in pairs]
        near = [lax.ppermute(a, "tm", pairs + back) for a in far]
        slots.append((lambda c, s=s: c - s, far))
        slots.append((lambda c, s=s: c + 1 - 2 * lax.rem(c, 2) - s, near))
    s = final - 1
    far = [lax.ppermute(a, "tm", [(1, final - 1)]) for a in own]
    near = [lax.ppermute(a, "tm", [(final - 1, final)]) for a in far]
    slots.append((lambda c: jnp.where(c >= final - 1, 1, -1), list(zip(near, far))))
    slots.append((lambda c: jnp.where(c == final, 0, -1), [a for _, a in held]))

    cuts = [len(groups) - 1 if i in (0, 1, len(slots) - 1) else len(groups) - 2 for i in range(len(slots))]
    early = [(origin, arrays[:cut]) for (origin, arrays), cut in zip(slots, cuts)]
    late = [(origin, arrays[cut:]) for (origin, arrays), cut in zip(slots, cuts)]
    states = {}
    for d in range(1, splits):
        states[d] = attend(q_parts[d], early, span_mask, None, False)

    columns = out_weight.shape[1]
    width = columns // COL_BLOCKS
    project = lambda a, w: jnp.dot(a, w, preferred_element_type=jnp.float32).astype(jnp.bfloat16)
    returned = [[] for _ in range(COL_BLOCKS)]
    for d in range(1, splits):
        attended = attend(q_parts[d], late, span_mask, states[d], True)
        back = [((i + d) % splits, i) for i in range(splits)]
        for j in range(COL_BLOCKS):
            partial = project(attended, out_weight[:, j * width : (j + 1) * width])
            returned[j].append(lax.ppermute(partial, "head", back))
    attended = attend(q_parts[0], slots, span_mask, None, True)
    kept = lax.optimization_barrier(project(attended, out_weight))
    updated = hidden
    for j in range(COL_BLOCKS):
        cols = slice(j * width, (j + 1) * width)
        total = kept[:, cols].astype(jnp.float32)
        for a in returned[j]:
            total = total + a.astype(jnp.float32)
        fresh = updated[:, cols].astype(jnp.float32) + gate_row[None, cols] * total
        updated = lax.dynamic_update_slice_in_dim(updated, fresh.astype(jnp.bfloat16), j * width, 1)
    return updated


def solution(mesh):
    sizes = (mesh.shape["tm"], mesh.shape["head"], mesh.shape["branch"])
    return jax.shard_map(
        functools.partial(body, sizes),
        mesh=mesh,
        in_specs=(
            P("branch", "tm", "head", None, None),
            P("branch", "tm", "head", None, None),
            P("branch", "tm", "head", None, None),
            P("tm", ("head", "branch"), None, None),
            P("tm", ("head", "branch"), None, None),
            P("branch", "tm", "head", None),
            P("head", None),
            P(),
            P(),
            P(),
            P(),
        ),
        out_specs=P("branch", "tm", "head", None),
        check_vma=False,
    )
```

```python
import functools
import math

import jax
import jax.numpy as jnp
from jax import lax
from jax.experimental import pallas as pl
from jax.experimental.pallas import tpu as pltpu
from jax.sharding import PartitionSpec as P

NEG_BIG = -1e30
LOG2E = 1.4426950408889634
COL_BLOCKS = 5
HEAD_STEP_SCORES = 1 << 20
VMEM_MARGIN = 3 << 20


def hidden_bias(mask, span, origin):
    source = origin(span)
    return jnp.where((source >= 0) & (mask[span, jnp.maximum(source, 0)] > 0), 0.0, NEG_BIG)


def flash_kernel(mask, *refs, layout, count, scale, step, first, last):
    q_ref, kv_refs, refs = refs[0], refs[1 : 1 + count], refs[1 + count :]
    span = lax.axis_index("tm")
    odd = lax.rem(span, 2) == 1
    biases = [None if origin is None else hidden_bias(mask, span, origin) for origin, _ in layout]

    def gather(kind, h):
        blocks = []
        for _, members in layout:
            for choices, _ in members:
                block = kv_refs[choices[0]][kind, h]
                if len(choices) > 1:
                    block = jnp.where(odd, block, kv_refs[choices[1]][kind, h])
                blocks.append(block)
        return jnp.concatenate(blocks, axis=0)

    if not first:
        (max_in, sum_in, acc_in), refs = refs[:3], refs[3:]
    outs, score_ref = refs[:-1], refs[-1]
    dim = q_ref.shape[2]
    order = [(bias, size) for bias, (_, members) in zip(biases, layout) for _, size in members]
    for h in range(step):
        raw = lax.dot_general(
            q_ref[h], gather(0, h), (((1,), (1,)), ((), ())), preferred_element_type=jnp.float32
        )
        at, top = 0, None
        for bias, size in order:
            for _ in range(0, size, dim):
                piece = raw[:, at : at + dim]
                if bias is not None:
                    piece = piece + bias
                score_ref[h, :, at : at + dim] = piece
                top = piece if top is None else jnp.maximum(top, piece)
                at += dim
        top = jnp.broadcast_to(jnp.max(top, axis=1, keepdims=True) * scale, top.shape)
        total = acc = None
        if not first:
            old = max_in[h]
            top = jnp.maximum(top, old)
            shrink = jnp.exp2(old - top)
            total, acc = sum_in[h] * shrink, acc_in[h] * shrink
        weights = []
        for j in range(0, at, dim):
            piece = jnp.exp2(score_ref[h, :, j : j + dim] * scale - top)
            total = piece if total is None else total + piece
            weights.append(piece.astype(jnp.bfloat16))
        added = jnp.dot(
            jnp.concatenate(weights, axis=1), gather(1, h), preferred_element_type=jnp.float32
        )
        acc = added if acc is None else acc + added
        if last:
            total = jnp.sum(total, axis=1, keepdims=True)
            outs[0][:, h * dim : (h + 1) * dim] = (acc / total).astype(outs[0].dtype)
        else:
            outs[0][h], outs[1][h], outs[2][h] = top, total, acc


def attend(queries, slots, span_mask, state, last):
    heads, rows, dim = queries.shape
    arrays, layout = [], []
    for origin, members in slots:
        places = []
        for member in members:
            choices = member if isinstance(member, tuple) else (member,)
            places.append((tuple(range(len(arrays), len(arrays) + len(choices))), choices[0].shape[2]))
            arrays += choices
        layout.append((origin, places))
    keys = sum(size for _, places in layout for _, size in places)
    step = max(s for s in range(1, heads + 1) if heads % s == 0 and s * rows * keys <= HEAD_STEP_SCORES)
    read = sum(array.shape[2] for array in arrays)
    blocks = step * dim * (2 * 2 * read + 2 * 2 * rows + 3 * 4 * rows)
    grant = 4 * step * rows * keys + 2 * blocks + VMEM_MARGIN
    by_head = pl.BlockSpec((step, rows, dim), lambda h, f: (h, 0, 0))
    states = [] if state is None else list(state)
    return pl.pallas_call(
        functools.partial(
            flash_kernel,
            layout=layout,
            count=len(arrays),
            scale=LOG2E / math.sqrt(dim),
            step=step,
            first=state is None,
            last=last,
        ),
        out_shape=jax.ShapeDtypeStruct((rows, heads * dim), jnp.bfloat16)
        if last
        else [jax.ShapeDtypeStruct((heads, rows, dim), jnp.float32)] * 3,
        grid_spec=pltpu.PrefetchScalarGridSpec(
            num_scalar_prefetch=1,
            grid=(heads // step,),
            in_specs=[by_head]
            + [
                pl.BlockSpec((2, step, array.shape[2], dim), lambda h, f: (0, h, 0, 0))
                for array in arrays
            ]
            + [by_head] * len(states),
            out_specs=pl.BlockSpec((rows, step * dim), lambda h, f: (0, h)) if last else [by_head] * 3,
            scratch_shapes=[pltpu.VMEM((step, rows, keys), jnp.float32)],
        ),
        cost_estimate=pl.CostEstimate(
            flops=4 * heads * rows * keys * dim,
            bytes_accessed=2 * heads * dim * (2 * rows + 2 * keys),
            transcendentals=heads * rows * keys,
        ),
        compiler_params=pltpu.CompilerParams(vmem_limit_bytes=grant),
    )(span_mask, queries, *arrays, *states)


def body(sizes, queries, keys, values, ctx_keys, ctx_values, hidden, out_weight, gates, levels, span_mask, prefix):
    return sublayer(
        sizes, queries[0, 0], keys[0, 0], values[0, 0], ctx_keys[0], ctx_values[0], hidden[0, 0],
        out_weight, gates, levels, span_mask, prefix,
    )[None, None]


def sublayer(sizes, queries, keys, values, ctx_keys, ctx_values, hidden, out_weight, gates, levels, span_mask, prefix):
    spans, splits, branches = sizes
    span = lax.axis_index("tm")
    part = lax.axis_index("head")
    to_heads = lambda a: jnp.transpose(a, (1, 0, 2))
    q, k, v = to_heads(queries), to_heads(keys), to_heads(values)
    ck, cv = to_heads(ctx_keys), to_heads(ctx_values)
    group = q.shape[0] // splits
    take = lambda a, d: lax.dynamic_slice_in_dim(a, lax.rem(part + d, splits) * group, group, 0)
    pair = lambda a, b, d: jnp.stack([take(a, d), take(b, d)])
    cycle = lambda d: [(i, (i + d) % splits) for i in range(splits)]


    ctx_parts, kv_parts, q_parts = [pair(ck, cv, 0)], [pair(k, v, 0)], [take(q, 0)]
    for d in range(1, splits):
        ctx_parts.append(lax.ppermute(pair(ck, cv, d), "head", cycle(d)))
    for d in range(1, splits):
        kv_parts.append(lax.ppermute(pair(k, v, d), "head", cycle(d)))
    for d in range(1, splits):
        q_parts.append(lax.ppermute(take(q, d), "head", cycle(d)))

    use_context = span < prefix[0]
    level_now = lax.dynamic_index_in_dim(levels, span, 0, keepdims=False)
    gate_row = lax.dynamic_index_in_dim(gates, level_now, 0, keepdims=False)
    final = spans - 1
    stands_in = span == final
    ctx_parts[0], gate_row = lax.optimization_barrier((ctx_parts[0], gate_row))
    lent = [lax.ppermute(a, "tm", [(0, final)]) for a in ctx_parts]
    pieces = [jnp.concatenate([jnp.where(stands_in, b, a) for a, b in zip(ctx_parts, lent)], axis=2)]
    piece_rows = pieces[0].shape[2]
    for i in range(1, branches):
        low = i & -i
        pieces.append(lax.ppermute(pieces[i - low], "branch", [(b, b ^ low) for b in range(branches)]))
    groups = [[i for i in range(branches) if i.bit_count() == n] for n in range(branches.bit_length())]
    rows, at, own, passed, held = k.shape[1], 0, [], [], []
    for members in groups:
        contexts = [pieces[i] for i in members]
        if own:
            held[-1], *contexts = lax.optimization_barrier(((own[-1], passed[-1]), *contexts))
        mine = []
        for _ in members:
            d, row = divmod(at, rows)
            mine.append(kv_parts[d][:, :, row : row + piece_rows])
            at += piece_rows
        context, mine = jnp.concatenate(contexts, axis=2), jnp.concatenate(mine, axis=2)
        own.append(jnp.where(use_context, context, mine))
        passed.append(jnp.where(use_context | stands_in, context, mine))
        held.append((own[-1], passed[-1]))

    pairs = [(i, i + 1) for i in range(0, spans, 2)]
    beside = [lax.ppermute(a, "tm", pairs + [(final, final - 1)]) for a in passed]
    slots = [
        (None, [a for a, _ in held]),
        (lambda c: jnp.where(lax.rem(c, 2) == 1, c - 1, jnp.where(c == final - 1, 0, -1)), beside),
    ]
    for s in range(2, final - 1, 2):
        far = [lax.ppermute(a, "tm", [(i, i + s) for i in range(spans - s)]) for a in own]
        back = [(b, a) for a, b in pairs]
        near = [lax.ppermute(a, "tm", pairs + back) for a in far]
        slots.append((lambda c, s=s: c - s, far))
        slots.append((lambda c, s=s: c + 1 - 2 * lax.rem(c, 2) - s, near))
    s = final - 1
    far = [lax.ppermute(a, "tm", [(1, final - 1)]) for a in own]
    near = [lax.ppermute(a, "tm", [(final - 1, final)]) for a in far]
    slots.append((lambda c: jnp.where(c >= final - 1, 1, -1), list(zip(near, far))))
    slots.append((lambda c: jnp.where(c == final, 0, -1), [a for _, a in held]))

    early = [(origin, arrays[:1]) for origin, arrays in slots]
    late = [(origin, arrays[1:]) for origin, arrays in slots]
    states = {}
    for d in range(1, splits):
        states[d] = attend(q_parts[d], early, span_mask, None, False)

    columns = out_weight.shape[1]
    width = columns // COL_BLOCKS
    project = lambda a, w: jnp.dot(a, w, preferred_element_type=jnp.float32).astype(jnp.bfloat16)
    returned = [[] for _ in range(COL_BLOCKS)]
    for d in range(1, splits):
        attended = attend(q_parts[d], late, span_mask, states[d], True)
        back = [((i + d) % splits, i) for i in range(splits)]
        for j in range(COL_BLOCKS):
            partial = project(attended, out_weight[:, j * width : (j + 1) * width])
            returned[j].append(lax.ppermute(partial, "head", back))
    attended = attend(q_parts[0], slots, span_mask, None, True)
    kept = lax.optimization_barrier(project(attended, out_weight))
    updated = hidden
    for j in range(COL_BLOCKS):
        cols = slice(j * width, (j + 1) * width)
        total = kept[:, cols].astype(jnp.float32)
        for a in returned[j]:
            total = total + a.astype(jnp.float32)
        fresh = updated[:, cols].astype(jnp.float32) + gate_row[None, cols] * total
        updated = lax.dynamic_update_slice_in_dim(updated, fresh.astype(jnp.bfloat16), j * width, 1)
    return updated


def solution(mesh):
    sizes = (mesh.shape["tm"], mesh.shape["head"], mesh.shape["branch"])
    return jax.shard_map(
        functools.partial(body, sizes),
        mesh=mesh,
        in_specs=(
            P("branch", "tm", "head", None, None),
            P("branch", "tm", "head", None, None),
            P("branch", "tm", "head", None, None),
            P("tm", ("head", "branch"), None, None),
            P("tm", ("head", "branch"), None, None),
            P("branch", "tm", "head", None),
            P("head", None),
            P(),
            P(),
            P(),
            P(),
        ),
        out_specs=P("branch", "tm", "head", None),
        check_vma=False,
    )
```

```python
import functools
import math

import jax
import jax.numpy as jnp
from jax import lax
from jax.experimental import pallas as pl
from jax.experimental.pallas import tpu as pltpu
from jax.sharding import PartitionSpec as P

NEG_BIG = -1e30
LOG2E = 1.4426950408889634
COL_BLOCKS = 2
ROW_BLOCKS = 2
HEAD_STEP_SCORES = 1 << 20
VMEM_MARGIN = 3 << 20


def hidden_bias(mask, span, origin):
    source = origin(span)
    return jnp.where((source >= 0) & (mask[span, jnp.maximum(source, 0)] > 0), 0.0, NEG_BIG)


def flash_kernel(mask, *refs, layout, count, scale, step, first, last):
    q_ref, kv_refs, refs = refs[0], refs[1 : 1 + count], refs[1 + count :]
    span = lax.axis_index("tm")
    odd = lax.rem(span, 2) == 1
    biases = [None if origin is None else hidden_bias(mask, span, origin) for origin, _ in layout]

    def gather(kind, h):
        blocks = []
        for _, members in layout:
            for choices, _ in members:
                block = kv_refs[choices[0]][kind, h]
                if len(choices) > 1:
                    block = jnp.where(odd, block, kv_refs[choices[1]][kind, h])
                blocks.append(block)
        return jnp.concatenate(blocks, axis=0)

    if not first:
        (max_in, sum_in, acc_in), refs = refs[:3], refs[3:]
    outs, score_ref = refs[:-1], refs[-1]
    dim = q_ref.shape[2]
    order = [(bias, size) for bias, (_, members) in zip(biases, layout) for _, size in members]
    for h in range(step):
        raw = lax.dot_general(
            q_ref[h], gather(0, h), (((1,), (1,)), ((), ())), preferred_element_type=jnp.float32
        )
        at, top = 0, None
        for bias, size in order:
            for _ in range(0, size, dim):
                piece = raw[:, at : at + dim]
                if bias is not None:
                    piece = piece + bias
                score_ref[h, :, at : at + dim] = piece
                top = piece if top is None else jnp.maximum(top, piece)
                at += dim
        top = jnp.broadcast_to(jnp.max(top, axis=1, keepdims=True) * scale, top.shape)
        total = acc = None
        if not first:
            old = max_in[h]
            top = jnp.maximum(top, old)
            shrink = jnp.exp2(old - top)
            total, acc = sum_in[h] * shrink, acc_in[h] * shrink
        weights = []
        for j in range(0, at, dim):
            piece = jnp.exp2(score_ref[h, :, j : j + dim] * scale - top)
            total = piece if total is None else total + piece
            weights.append(piece.astype(jnp.bfloat16))
        added = jnp.dot(
            jnp.concatenate(weights, axis=1), gather(1, h), preferred_element_type=jnp.float32
        )
        acc = added if acc is None else acc + added
        if last:
            total = jnp.sum(total, axis=1, keepdims=True)
            outs[0][:, h * dim : (h + 1) * dim] = (acc / total).astype(outs[0].dtype)
        else:
            outs[0][h], outs[1][h], outs[2][h] = top, total, acc


def attend(queries, slots, span_mask, state, last, share=(0, 1)):
    heads, rows, dim = queries.shape
    rows, at_row = rows // share[1], share[0]
    arrays, layout = [], []
    for origin, members in slots:
        places = []
        for member in members:
            choices = member if isinstance(member, tuple) else (member,)
            places.append((tuple(range(len(arrays), len(arrays) + len(choices))), choices[0].shape[2]))
            arrays += choices
        layout.append((origin, places))
    keys = sum(size for _, places in layout for _, size in places)
    step = max(s for s in range(1, heads + 1) if heads % s == 0 and s * rows * keys <= HEAD_STEP_SCORES)
    read = sum(array.shape[2] for array in arrays)
    blocks = step * dim * (2 * 2 * read + 2 * 2 * rows + 3 * 4 * rows)
    grant = 4 * step * rows * keys + 2 * blocks + VMEM_MARGIN
    by_head = pl.BlockSpec((step, rows, dim), lambda h, f: (h, at_row, 0))
    states = [] if state is None else list(state)
    return pl.pallas_call(
        functools.partial(
            flash_kernel,
            layout=layout,
            count=len(arrays),
            scale=LOG2E / math.sqrt(dim),
            step=step,
            first=state is None,
            last=last,
        ),
        out_shape=jax.ShapeDtypeStruct((rows, heads * dim), jnp.bfloat16)
        if last
        else [jax.ShapeDtypeStruct((heads, rows, dim), jnp.float32)] * 3,
        grid_spec=pltpu.PrefetchScalarGridSpec(
            num_scalar_prefetch=1,
            grid=(heads // step,),
            in_specs=[by_head]
            + [
                pl.BlockSpec((2, step, array.shape[2], dim), lambda h, f: (0, h, 0, 0))
                for array in arrays
            ]
            + [by_head] * len(states),
            out_specs=pl.BlockSpec((rows, step * dim), lambda h, f: (0, h)) if last else [by_head] * 3,
            scratch_shapes=[pltpu.VMEM((step, rows, keys), jnp.float32)],
        ),
        cost_estimate=pl.CostEstimate(
            flops=4 * heads * rows * keys * dim,
            bytes_accessed=2 * heads * dim * (2 * rows + 2 * keys),
            transcendentals=heads * rows * keys,
        ),
        compiler_params=pltpu.CompilerParams(vmem_limit_bytes=grant),
    )(span_mask, queries, *arrays, *states)


def body(sizes, queries, keys, values, ctx_keys, ctx_values, hidden, out_weight, gates, levels, span_mask, prefix):
    return sublayer(
        sizes, queries[0, 0], keys[0, 0], values[0, 0], ctx_keys[0], ctx_values[0], hidden[0, 0],
        out_weight, gates, levels, span_mask, prefix,
    )[None, None]


def sublayer(sizes, queries, keys, values, ctx_keys, ctx_values, hidden, out_weight, gates, levels, span_mask, prefix):
    spans, splits, branches = sizes
    span = lax.axis_index("tm")
    part = lax.axis_index("head")
    to_heads = lambda a: jnp.transpose(a, (1, 0, 2))
    q, k, v = to_heads(queries), to_heads(keys), to_heads(values)
    ck, cv = to_heads(ctx_keys), to_heads(ctx_values)
    group = q.shape[0] // splits
    take = lambda a, d: lax.dynamic_slice_in_dim(a, lax.rem(part + d, splits) * group, group, 0)
    pair = lambda a, b, d: jnp.stack([take(a, d), take(b, d)])
    cycle = lambda d: [(i, (i + d) % splits) for i in range(splits)]


    ctx_parts, kv_parts, q_parts = [pair(ck, cv, 0)], [pair(k, v, 0)], [take(q, 0)]
    for d in range(1, splits):
        ctx_parts.append(lax.ppermute(pair(ck, cv, d), "head", cycle(d)))
    for d in range(1, splits):
        kv_parts.append(lax.ppermute(pair(k, v, d), "head", cycle(d)))
    for d in range(1, splits):
        q_parts.append(lax.ppermute(take(q, d), "head", cycle(d)))

    use_context = span < prefix[0]
    level_now = lax.dynamic_index_in_dim(levels, span, 0, keepdims=False)
    gate_row = lax.dynamic_index_in_dim(gates, level_now, 0, keepdims=False)
    final = spans - 1
    stands_in = span == final
    ctx_parts[0], gate_row = lax.optimization_barrier((ctx_parts[0], gate_row))
    lent = [lax.ppermute(a, "tm", [(0, final)]) for a in ctx_parts]
    pieces = [jnp.concatenate([jnp.where(stands_in, b, a) for a, b in zip(ctx_parts, lent)], axis=2)]
    piece_rows = pieces[0].shape[2]
    for i in range(1, branches):
        low = i & -i
        pieces.append(lax.ppermute(pieces[i - low], "branch", [(b, b ^ low) for b in range(branches)]))
    groups = [[i for i in range(branches) if i.bit_count() == n] for n in range(branches.bit_length())]
    rows, at, own, passed, held = k.shape[1], 0, [], [], []
    for members in groups:
        contexts = [pieces[i] for i in members]
        if own:
            held[-1], *contexts = lax.optimization_barrier(((own[-1], passed[-1]), *contexts))
        mine = []
        for _ in members:
            d, row = divmod(at, rows)
            mine.append(kv_parts[d][:, :, row : row + piece_rows])
            at += piece_rows
        context, mine = jnp.concatenate(contexts, axis=2), jnp.concatenate(mine, axis=2)
        own.append(jnp.where(use_context, context, mine))
        passed.append(jnp.where(use_context | stands_in, context, mine))
        held.append((own[-1], passed[-1]))

    pairs = [(i, i + 1) for i in range(0, spans, 2)]
    beside = [lax.ppermute(a, "tm", pairs + [(final, final - 1)]) for a in passed]
    slots = [
        (None, [a for a, _ in held]),
        (lambda c: jnp.where(lax.rem(c, 2) == 1, c - 1, jnp.where(c == final - 1, 0, -1)), beside),
    ]
    for s in range(2, final - 1, 2):
        far = [lax.ppermute(a, "tm", [(i, i + s) for i in range(spans - s)]) for a in own]
        back = [(b, a) for a, b in pairs]
        near = [lax.ppermute(a, "tm", pairs + back) for a in far]
        slots.append((lambda c, s=s: c - s, far))
        slots.append((lambda c, s=s: c + 1 - 2 * lax.rem(c, 2) - s, near))
    s = final - 1
    far = [lax.ppermute(a, "tm", [(1, final - 1)]) for a in own]
    near = [lax.ppermute(a, "tm", [(final - 1, final)]) for a in far]
    slots.append((lambda c: jnp.where(c >= final - 1, 1, -1), list(zip(near, far))))
    slots.append((lambda c: jnp.where(c == final, 0, -1), [a for _, a in held]))

    cuts = [len(groups) - 1 if i in (0, 1, len(slots) - 1) else len(groups) - 2 for i in range(len(slots))]
    early = [(origin, arrays[:cut]) for (origin, arrays), cut in zip(slots, cuts)]
    late = [(origin, arrays[cut:]) for (origin, arrays), cut in zip(slots, cuts)]
    states = {}
    for d in range(1, splits):
        states[d] = attend(q_parts[d], early, span_mask, None, False)

    columns = out_weight.shape[1]
    width = columns // COL_BLOCKS
    project = lambda a, w: jnp.dot(a, w, preferred_element_type=jnp.float32).astype(jnp.bfloat16)
    height = q.shape[1] // ROW_BLOCKS
    tiles = [(r, j) for r in range(ROW_BLOCKS) for j in range(COL_BLOCKS)]
    returned = {tile: [] for tile in tiles}
    for d in range(1, splits):
        back = [((i + d) % splits, i) for i in range(splits)]
        for r, j in tiles:
            if j == 0:
                attended = attend(q_parts[d], late, span_mask, states[d], True, (r, ROW_BLOCKS))
            partial = project(attended, out_weight[:, j * width : (j + 1) * width])
            returned[r, j].append(lax.ppermute(partial, "head", back))
    attended = attend(q_parts[0], slots, span_mask, None, True)
    kept = lax.optimization_barrier(project(attended, out_weight))
    updated = hidden
    for r, j in tiles:
        block = slice(r * height, (r + 1) * height), slice(j * width, (j + 1) * width)
        total = kept[block].astype(jnp.float32)
        for a in returned[r, j]:
            total = total + a.astype(jnp.float32)
        fresh = updated[block].astype(jnp.float32) + gate_row[None, block[1]] * total
        updated = lax.dynamic_update_slice(updated, fresh.astype(jnp.bfloat16), (r * height, j * width))
    return updated


def solution(mesh):
    sizes = (mesh.shape["tm"], mesh.shape["head"], mesh.shape["branch"])
    return jax.shard_map(
        functools.partial(body, sizes),
        mesh=mesh,
        in_specs=(
            P("branch", "tm", "head", None, None),
            P("branch", "tm", "head", None, None),
            P("branch", "tm", "head", None, None),
            P("tm", ("head", "branch"), None, None),
            P("tm", ("head", "branch"), None, None),
            P("branch", "tm", "head", None),
            P("head", None),
            P(),
            P(),
            P(),
            P(),
        ),
        out_specs=P("branch", "tm", "head", None),
        check_vma=False,
    )
```
